512 devices in a mesh: grp: 16 (over y_lo, z), sub: 32 (over y_hi, x, core).
Axes of the slice: x: 4, y: 8 (y_hi: 4, y_lo: 2; y = y_hi * 2 + y_lo), z: 8, core: 2. Of those that a mesh axis runs over, the one named last changes fastest.
Arguments:
- phase_labels: int32 [512, 1152], P(('grp', 'sub')), may hold values from 0 to 2
- phase_perm: float32 [3], replicated, may hold values from 0.2 to 5
- local_inverse: bfloat16 [512, 1152, 1152], P(('grp', 'sub')), may hold values from -0.1875 to 0.1875
- sources: bfloat16 [512, 256, 1152], P(('grp', 'sub')), may hold values from -6 to 6
- shift: float32 [512, 256], P(('grp', 'sub')), may hold values from 1 to 30
- probe: float32 [256, 8], replicated, may hold values from -48 to 48
Outputs:
- coefficients: float32 [512, 256, 8], P(('grp', 'sub'))
- element_stiffness: float32 [512, 32, 32], P(('grp', 'sub'))
The draws below stay inside these ranges and needn't reach their ends.
All inputs are finite; a program needn't handle non-finite values.
Results may differ from the reference program's by a relative error of at most 0.0055.
Values may be sent and summed in bfloat16 or wider, within the bound.
A program may use at most 64 MiB of HBM per device.

```python
import math
import jax
import jax.numpy as jnp
from jax import lax

CELLX = 12
CELLY = 12
CELLZ = 8
SNAP = 256
NBASIS = 8
PHASES = 3
NCELL = 1152
BLOCKS = 512
NODES = 512
N_GRP = 16
N_SUB = 32


def touch_ends(array, key, low, largest):
    index_at = [jax.random.randint(jax.random.fold_in(key, axis), (), 0, length) for axis, length in enumerate(array.shape)]
    longest = array.shape.index(max(array.shape))
    neighbour = index_at[:longest] + [(index_at[longest] + 1) % array.shape[longest]] + index_at[longest + 1:]
    return array.at[tuple(index_at)].set(low).at[tuple(neighbour)].set(largest)


def level_of(own_key, shape, split, least, largest):
    loudness, own = 1.0, jax.random.fold_in(own_key, 6)
    for dim, blocks in split:
        heights = jnp.exp(jax.random.uniform(jax.random.fold_in(own, dim), (blocks,), jnp.float32, least / len(split), largest / len(split)))
        loudness = loudness * jnp.repeat(heights, shape[dim] // blocks).reshape([-1 if axis == dim else 1 for axis in range(len(shape))])
    return loudness


def gaussian(stream_key, extent, deviation, most, split=(), kind=jnp.bfloat16):
    result = deviation * jax.random.normal(stream_key, extent, jnp.float32)
    if split:
        result = result * level_of(stream_key, extent, split, -0.22, 0.18)
    return jnp.clip(result, -most, most).astype(kind)


def setup_inputs(seed: int = 0) -> dict:
    key_list = jax.random.split(jax.random.key(seed), 7)
    return {
        "phase_labels": touch_ends(jax.random.randint(key_list[0], (BLOCKS, NCELL), 0, 3), jax.random.fold_in(key_list[0], 1), 0, 2).astype(jnp.int32),
        "phase_perm": jnp.clip(jnp.exp(jax.random.uniform(key_list[1], (PHASES,), jnp.float32, math.log(0.2), math.log(5.0))), 0.2, 5.0),
        "local_inverse": gaussian(key_list[2], (BLOCKS, NCELL, NCELL), NCELL ** -0.5, 0.1875, ((0, 512),)),
        "sources": gaussian(key_list[3], (BLOCKS, SNAP, NCELL), 1.0, 6.0, ((0, 512),)),
        "shift": jnp.clip(jnp.exp(math.log(30.0) - 3.4011974 * jax.random.uniform(key_list[4], (NODES, SNAP), jnp.float32) ** level_of(key_list[4], (NODES, SNAP), ((0, 512),), -0.2, 0.2)), 1.0, 30.0),
        "probe": gaussian(key_list[5], (SNAP, NBASIS), 8.0, 48.0, (), jnp.float32),
    }


HIGH_PRECISION = lax.Precision.HIGHEST

def weights_of(material_labels, phase_perm):
    cell_index = jnp.arange(NCELL, dtype=jnp.int32)
    coord_x = cell_index // (CELLY * CELLZ)
    coord_y = cell_index // CELLZ % CELLY
    coord_z = cell_index % CELLZ
    frac_x = (coord_x.astype(jnp.float32) + 0.5) / CELLX
    frac_y = (coord_y.astype(jnp.float32) + 0.5) / CELLY
    partition = jnp.stack([(1.0 - frac_x) * (1.0 - frac_y), frac_x * (1.0 - frac_y), (1.0 - frac_x) * frac_y, frac_x * frac_y])
    onehot = (material_labels[None, :] == jnp.arange(PHASES, dtype=jnp.int32)[:, None]).astype(jnp.float32)
    cell_permeability = jnp.sum(onehot * phase_perm[:, None], axis=0)
    face_list = []
    weight_list = []
    for stride, coordinate, limit in ((CELLY * CELLZ, coord_x, CELLX), (CELLZ, coord_y, CELLY), (1, coord_z, CELLZ)):
        neighbour_permeability = jnp.roll(cell_permeability, -stride)
        inside = (coordinate < limit - 1).astype(jnp.float32)
        face_kappa = 2.0 * cell_permeability * neighbour_permeability / (cell_permeability + neighbour_permeability) * inside
        face_list.append(face_kappa)
        weight_list.append(face_kappa[None, :] * 0.5 * (partition + jnp.roll(partition, -stride, axis=1)))
    return (partition, jnp.stack(face_list), cell_permeability[None, :] * partition, jnp.stack(weight_list))

def differences(field):
    return jnp.stack([jnp.roll(field, -stride, axis=-1) - field for stride in (CELLY * CELLZ, CELLZ, 1)])

def reference(phase_labels, phase_perm, local_inverse, sources, shift, probe):
    volume = 1.0 / NCELL

    def snapshots_of(inverse, source_rows):
        return jnp.dot(source_rows.astype(jnp.float32), inverse.astype(jnp.float32), preferred_element_type=jnp.float32).astype(jnp.bfloat16)

    def block_grams(packed):
        material_labels, inverse, source_rows = packed
        partition, face_kappa, mass_weight, face_weight = weights_of(material_labels, phase_perm)
        snapshot_fields = snapshots_of(inverse, source_rows)
        gradients = differences(snapshot_fields.astype(jnp.float32)).astype(jnp.bfloat16)
        mass_weighted = (snapshot_fields.astype(jnp.float32)[None] * (mass_weight * volume)[:, None, :]).astype(jnp.bfloat16)
        mass_gram = jnp.einsum('csn,tn->cst', mass_weighted.astype(jnp.float32), snapshot_fields.astype(jnp.float32), precision=HIGH_PRECISION)
        grad_weighted = (gradients.astype(jnp.float32)[:, None] * (face_weight * volume)[:, :, None, :]).astype(jnp.bfloat16)
        stiffness = jnp.einsum('dcsn,dtn->cst', grad_weighted.astype(jnp.float32), gradients.astype(jnp.float32), precision=HIGH_PRECISION)
        return (mass_gram, stiffness)
    mass_gram, stiffness = lax.map(block_grams, (phase_labels, local_inverse, sources))

    def to_nodes(gram_set):
        block_grid = gram_set.reshape(N_GRP, N_SUB, 4, SNAP, SNAP)
        node_total = block_grid[:, :, 0] + jnp.roll(block_grid[:, :, 1], 1, axis=1)
        node_total = node_total + jnp.roll(block_grid[:, :, 2], 1, axis=0)
        node_total = node_total + jnp.roll(jnp.roll(block_grid[:, :, 3], 1, axis=0), 1, axis=1)
        return node_total.reshape(NODES, SNAP, SNAP)
    node_mass = to_nodes(mass_gram)
    node_stiff = to_nodes(stiffness)

    def solve_node(packed):
        stiff_node, mass_node, shift_node = packed
        right_side = jnp.dot(mass_node, probe, precision=HIGH_PRECISION)
        cholesky_factor = jnp.linalg.cholesky(stiff_node + jnp.diag(shift_node))
        return jax.scipy.linalg.cho_solve((cholesky_factor, True), right_side)
    coefficients = lax.map(solve_node, (node_stiff, node_mass, shift))
    coef_grid = coefficients.reshape(N_GRP, N_SUB, SNAP, NBASIS)
    right_coef = jnp.roll(coef_grid, -1, axis=1)
    upper_coef = jnp.roll(coef_grid, -1, axis=0)
    diagonal_coef = jnp.roll(right_coef, -1, axis=0)
    corner_all = jnp.stack([coef_grid, right_coef, upper_coef, diagonal_coef], axis=2).reshape(BLOCKS, 4, SNAP, NBASIS)

    def element(packed):
        material_labels, inverse, source_rows, corner_coefficient = packed
        partition, face_kappa, mass_weight, face_weight = weights_of(material_labels, phase_perm)
        snapshot_fields = snapshots_of(inverse, source_rows)
        corner_coefficient = corner_coefficient.astype(jnp.bfloat16)
        field_projection = jnp.einsum('wrp,rd->wpd', corner_coefficient.astype(jnp.float32), snapshot_fields.astype(jnp.float32), precision=HIGH_PRECISION)
        basis_field = (field_projection * partition[:, None, :]).reshape(4 * NBASIS, NCELL)
        slopes = differences(basis_field)
        return jnp.einsum('dan,dbn->ab', slopes * face_kappa[:, None, :], slopes, precision=HIGH_PRECISION) / (NCELL * SNAP)
    element_stiffness = lax.map(element, (phase_labels, local_inverse, sources, corner_all))
    return (coefficients, element_stiffness)
```

```python
import jax
import jax.numpy as jnp
from jax import lax
from jax.experimental import pallas as pl
from jax.experimental.pallas import tpu as pltpu
from jax.sharding import PartitionSpec as P

CELLX = 12
CELLY = 12
CELLZ = 8
SNAP = 256
NBASIS = 8
PHASES = 3
NCELL = 1152


HIGH_PRECISION = lax.Precision.HIGHEST
HI = HIGH_PRECISION
N = SNAP
NB = 16
W = 384


def leaf(cols, slabs, nb):
    rows = lax.broadcasted_iota(jnp.int32, (nb, 128), 0)
    cols = list(cols)
    slabs = list(slabs)
    for p in range(0, nb, 2):
        c0, c1 = cols[p], cols[p + 1]
        a, b = c0[p:p + 1], c1[p:p + 1]
        bt, d = c0[p + 1:p + 2], c1[p + 1:p + 2]
        inv = 1.0 / (a * d - b * bt)
        a, b, bt, d = a * inv, b * inv, bt * inv, d * inv
        top, bottom = rows == p, rows == p + 1
        def step(t):
            r0, r1 = t[p:p + 1], t[p + 1:p + 2]
            s0 = d * r0 - b * r1
            s1 = a * r1 - bt * r0
            return jnp.where(top, s0, jnp.where(bottom, s1, t - c0 * s0 - c1 * s1))
        for q in range(p + 2, nb):
            cols[q] = step(cols[q])
        slabs = [step(t) for t in slabs]
    return slabs

def solver_kernel(k_ref, shift_ref, rhs_ref, out_ref, m_ref):
    nb = NB
    ri = lax.broadcasted_iota(jnp.int32, (N, N), 0)
    ci = lax.broadcasted_iota(jnp.int32, (N, N), 1)
    m_ref[:, :N] = k_ref[...] + jnp.where(ri == ci, shift_ref[...], 0.0)
    m_ref[:, N:] = jnp.zeros((N, 128), jnp.float32)
    m_ref[:, N:N + 8] = rhs_ref[...]
    steps = N // nb
    tile = lambda k: (k * nb) // 128
    slab = [m_ref[0:nb, 128 * t:128 * t + 128] for t in range(3)]
    for k in range(steps):
        t0, off = tile(k), (k * nb) % 128
        diag = slab[t0]
        cols = [jnp.broadcast_to(diag[:, off + q:off + q + 1], (nb, 128)) for q in range(nb)]
        live = [t for t in range(3) if t == 2 or (t >= tile(k + 1) and k + 1 < steps)]
        new = leaf(cols, [slab[t] for t in live], nb)
        new = dict(zip(live, new))
        wide = jnp.concatenate([new[t] for t in live], axis=1)
        before, after = off, 128 - off - nb
        pieces = ([jnp.zeros((before, 128 * len(live)), jnp.float32)] if before else []) + [wide] + (
            [jnp.zeros((after, 128 * len(live)), jnp.float32)] if after else [])
        padded = jnp.concatenate(pieces, axis=0)
        lo = live[0] * 128
        def update(r0, r1):
            left = m_ref[r0:r1, 128 * t0:128 * t0 + 128]
            return m_ref[r0:r1, lo:] - jnp.dot(left, padded, precision=HI, preferred_element_type=jnp.float32)
        if k + 1 < steps:
            nxt = update((k + 1) * nb, (k + 2) * nb)
            for i, t in enumerate(live):
                new[t] = nxt[:, 128 * i:128 * i + 128]
            newslab = [new.get(t) for t in range(3)]
            if k + 2 < steps:
                m_ref[(k + 2) * nb:, lo:] = update((k + 2) * nb, N)
        if k > 0:
            m_ref[:k * nb, lo:] = update(0, k * nb)
        m_ref[k * nb:(k + 1) * nb, lo:] = wide
        if k + 1 < steps:
            slab = newslab
    out_ref[...] = m_ref[:, N:N + 8]

def solve(k, shift, rhs):
    return pl.pallas_call(
        solver_kernel,
        out_shape=jax.ShapeDtypeStruct((N, 8), jnp.float32),
        in_specs=[pl.BlockSpec(memory_space=pltpu.VMEM)] * 3,
        out_specs=pl.BlockSpec(memory_space=pltpu.VMEM),
        scratch_shapes=[pltpu.VMEM((N, W), jnp.float32)],
        name="solver",
    )(k, shift, rhs)


def passed_along(block, axis, distance):
    devices = range(lax.axis_size(axis))
    route = [((i - distance) % len(devices), i) for i in devices]
    return lax.ppermute(block, axis, route)


def weights_of(material_labels, phase_perm):
    cell_index = jnp.arange(NCELL, dtype=jnp.int32)
    coord_x = cell_index // (CELLY * CELLZ)
    coord_y = cell_index // CELLZ % CELLY
    coord_z = cell_index % CELLZ
    frac_x = (coord_x.astype(jnp.float32) + 0.5) / CELLX
    frac_y = (coord_y.astype(jnp.float32) + 0.5) / CELLY
    partition = jnp.stack(
        [
            (1.0 - frac_x) * (1.0 - frac_y),
            frac_x * (1.0 - frac_y),
            (1.0 - frac_x) * frac_y,
            frac_x * frac_y,
        ]
    )
    onehot = (material_labels[None, :] == jnp.arange(PHASES, dtype=jnp.int32)[:, None]).astype(
        jnp.float32
    )
    cell_permeability = jnp.sum(onehot * phase_perm[:, None], axis=0)
    face_list = []
    weight_list = []
    for stride, coordinate, limit in (
        (CELLY * CELLZ, coord_x, CELLX),
        (CELLZ, coord_y, CELLY),
        (1, coord_z, CELLZ),
    ):
        neighbour_permeability = jnp.roll(cell_permeability, -stride)
        inside = (coordinate < limit - 1).astype(jnp.float32)
        face_kappa = (
            2.0
            * cell_permeability
            * neighbour_permeability
            / (cell_permeability + neighbour_permeability)
            * inside
        )
        face_list.append(face_kappa)
        weight_list.append(
            face_kappa[None, :] * 0.5 * (partition + jnp.roll(partition, -stride, axis=1))
        )
    return (
        partition,
        jnp.stack(face_list),
        cell_permeability[None, :] * partition,
        jnp.stack(weight_list),
    )


def differences(field):
    return jnp.stack(
        [jnp.roll(field, -stride, axis=-1) - field for stride in (CELLY * CELLZ, CELLZ, 1)]
    )


def local(phase_labels, phase_perm, local_inverse, sources, shift, probe):
    volume = 1.0 / NCELL
    partition, face_kappa, mass_weight, face_weight = weights_of(phase_labels[0], phase_perm)
    snapshot_fields = jnp.dot(
        sources[0], local_inverse[0], preferred_element_type=jnp.float32
    ).astype(jnp.bfloat16)
    gradients = differences(snapshot_fields.astype(jnp.float32)).astype(jnp.bfloat16)
    fields = snapshot_fields.astype(jnp.float32)
    probed = jnp.dot(probe.T, fields, precision=HIGH_PRECISION)
    loads = ((mass_weight * volume)[:, None, :] * probed).reshape(4 * NBASIS, NCELL)
    corner_side = jnp.einsum("an,sn->as", loads, fields, precision=HIGH_PRECISION).reshape(4, NBASIS, SNAP)
    grad_weighted = (gradients[:, None] * (face_weight * volume)[:, :, None, :]).astype(
        jnp.bfloat16
    )
    stiffness = jnp.einsum(
        "dcsn,dtn->cst", grad_weighted, gradients, preferred_element_type=jnp.float32
    )
    bf = jnp.bfloat16
    came_stiff, came_side = passed_along((stiffness[1::2].astype(bf), corner_side[1::2]), "sub", 1)
    row_stiff = stiffness[0::2] + came_stiff.astype(jnp.float32)
    row_side = corner_side[0::2] + came_side
    below_stiff, below_side = passed_along((row_stiff[1].astype(bf), row_side[1]), "grp", 1)
    node_stiff = row_stiff[0] + below_stiff.astype(jnp.float32)
    right_side = (row_side[0] + below_side).T
    coefficients = solve(node_stiff, shift, right_side)
    own_coef = coefficients.astype(jnp.bfloat16)
    upper_coef = passed_along(own_coef, "grp", -1)
    right_coef, diagonal_coef = passed_along((own_coef, upper_coef), "sub", -1)
    corner_coefficient = jnp.stack([own_coef, right_coef, upper_coef, diagonal_coef])
    field_projection = jnp.einsum(
        "wrp,rd->wpd", corner_coefficient, snapshot_fields, preferred_element_type=jnp.float32
    )
    basis_field = (field_projection * partition[:, None, :]).reshape(4 * NBASIS, NCELL)
    slopes = differences(basis_field)
    element_stiffness = jnp.einsum(
        "dan,dbn->ab", slopes * face_kappa[:, None, :], slopes, precision=HIGH_PRECISION
    ) / (NCELL * SNAP)
    return (coefficients[None], element_stiffness[None])


def solution(mesh):
    in_specs = (
        P(("grp", "sub"), None),
        P(),
        P(("grp", "sub"), None, None),
        P(("grp", "sub"), None, None),
        P(("grp", "sub"), None),
        P(),
    )
    out_specs = (P(("grp", "sub"), None, None), P(("grp", "sub"), None, None))
    return jax.shard_map(local, mesh=mesh, in_specs=in_specs, out_specs=out_specs, check_vma=False)
```

```python
import functools
import jax
import jax.numpy as jnp
from jax import lax
from jax.experimental import pallas as pl
from jax.experimental.pallas import tpu as pltpu
from jax.sharding import PartitionSpec as P

HI = lax.Precision.HIGHEST
N = 256
NB = 16
W = 384

def leaf(cols, slabs, nb):
    rows = lax.broadcasted_iota(jnp.int32, (nb, 128), 0)
    cols = list(cols)
    slabs = list(slabs)
    for p in range(0, nb, 2):
        c0, c1 = cols[p], cols[p + 1]
        a, b = c0[p:p + 1], c1[p:p + 1]
        bt, d = c0[p + 1:p + 2], c1[p + 1:p + 2]
        inv = 1.0 / (a * d - b * bt)
        a, b, bt, d = a * inv, b * inv, bt * inv, d * inv
        top, bottom = rows == p, rows == p + 1
        def step(t):
            r0, r1 = t[p:p + 1], t[p + 1:p + 2]
            s0 = d * r0 - b * r1
            s1 = a * r1 - bt * r0
            return jnp.where(top, s0, jnp.where(bottom, s1, t - c0 * s0 - c1 * s1))
        for q in range(p + 2, nb):
            cols[q] = step(cols[q])
        slabs = [step(t) for t in slabs]
    return slabs

def solver_kernel(k_ref, shift_ref, rhs_ref, out_ref, m_ref):
    nb = NB
    ri = lax.broadcasted_iota(jnp.int32, (N, N), 0)
    ci = lax.broadcasted_iota(jnp.int32, (N, N), 1)
    m_ref[:, :N] = k_ref[...] + jnp.where(ri == ci, shift_ref[...], 0.0)
    m_ref[:, N:] = jnp.zeros((N, 128), jnp.float32)
    m_ref[:, N:N + 8] = rhs_ref[...].T
    steps = N // nb
    tile = lambda k: (k * nb) // 128
    slab = [m_ref[0:nb, 128 * t:128 * t + 128] for t in range(3)]
    for k in range(steps):
        t0, off = tile(k), (k * nb) % 128
        diag = slab[t0]
        cols = [jnp.broadcast_to(diag[:, off + q:off + q + 1], (nb, 128)) for q in range(nb)]
        live = [t for t in range(3) if t == 2 or (t >= tile(k + 1) and k + 1 < steps)]
        new = leaf(cols, [slab[t] for t in live], nb)
        new = dict(zip(live, new))
        wide = jnp.concatenate([new[t] for t in live], axis=1)
        before, after = off, 128 - off - nb
        pieces = ([jnp.zeros((before, 128 * len(live)), jnp.float32)] if before else []) + [wide] + (
            [jnp.zeros((after, 128 * len(live)), jnp.float32)] if after else [])
        padded = jnp.concatenate(pieces, axis=0)
        lo = live[0] * 128
        def update(r0, r1):
            left = m_ref[r0:r1, 128 * t0:128 * t0 + 128]
            return m_ref[r0:r1, lo:] - jnp.dot(left, padded, precision=HI, preferred_element_type=jnp.float32)
        if k + 1 < steps:
            nxt = update((k + 1) * nb, (k + 2) * nb)
            for i, t in enumerate(live):
                new[t] = nxt[:, 128 * i:128 * i + 128]
            newslab = [new.get(t) for t in range(3)]
            if k + 2 < steps:
                m_ref[(k + 2) * nb:, lo:] = update((k + 2) * nb, N)
        if k > 0:
            m_ref[:k * nb, lo:] = update(0, k * nb)
        m_ref[k * nb:(k + 1) * nb, lo:] = wide
        if k + 1 < steps:
            slab = newslab
    out_ref[0] = m_ref[:, N:N + 8]

def solve(k, shift, rhs):
    return pl.pallas_call(
        solver_kernel,
        out_shape=jax.ShapeDtypeStruct((1, N, 8), jnp.float32),
        in_specs=[pl.BlockSpec(memory_space=pltpu.VMEM)] * 3,
        out_specs=pl.BlockSpec(memory_space=pltpu.VMEM),
        scratch_shapes=[pltpu.VMEM((N, W), jnp.float32)],
        name="solver",
    )(k, shift, rhs)


CELLX, CELLY, CELLZ, SNAP, NBASIS, PHASES, NCELL = 12, 12, 8, 256, 8, 3, 1152
STRIDES = (CELLY * CELLZ, CELLZ, 1)
CHUNKS = 3
PACK = 416
MESH = pl.DeviceIdType.MESH
NT = (((1,), (1,)), ((), ()))
VMEM = pl.BlockSpec(memory_space=pltpu.VMEM)
bf, f32 = jnp.bfloat16, jnp.float32


def ahead(field, stride):
    return pltpu.roll(field, NCELL - stride, axis=1)


def cell_weights():
    cell = lax.broadcasted_iota(jnp.int32, (1, NCELL), 1)
    run = lax.shift_right_logical(cell, 3)
    coord_x = lax.shift_right_logical(run * 683, 13)
    coord_y = run - coord_x * CELLY
    coord_z = lax.bitwise_and(cell, CELLZ - 1)
    fx = (coord_x.astype(f32) + 0.5) * (1.0 / CELLX)
    fy = (coord_y.astype(f32) + 0.5) * (1.0 / CELLY)
    partition = [(1.0 - fx) * (1.0 - fy), fx * (1.0 - fy), (1.0 - fx) * fy, fx * fy]
    inside = [coord_x < CELLX - 1, coord_y < CELLY - 1, coord_z < CELLZ - 1]
    return partition, inside


def permeability(labels_ref, perm_ref, inside):
    labels = labels_ref[...]
    kappa = jnp.where(labels == 0, perm_ref[0], jnp.where(labels == 1, perm_ref[1], perm_ref[2]))
    face = []
    for stride, keep in zip(STRIDES, inside):
        other = ahead(kappa, stride)
        face.append(jnp.where(keep, 2.0 * kappa * other / (kappa + other), 0.0))
    return kappa, face


def split3(x):
    hi = x.astype(bf)
    rest = x - hi.astype(f32)
    mid = rest.astype(bf)
    low = (rest - mid.astype(f32)).astype(bf)
    return jnp.concatenate([hi, mid, low], axis=0)


def neighbours(axes_size, step):
    grps, subs = axes_size
    g, s = lax.axis_index("grp"), lax.axis_index("sub")
    g1 = lax.rem(g + grps + step, grps)
    s1 = lax.rem(s + subs + step, subs)
    return [(g, s1), (g1, s), (g1, s1)]


def front_kernel(size, labels_ref, perm_ref, inverse_ref, sources_ref, probe_ref,
                 snap_ref, stiff_ref, side_ref, inv_ref, grad_ref, out_ref, in_ref,
                 load_sem, send_sem, recv_sem):
    rows = NCELL // CHUNKS
    loads = []
    for i in range(CHUNKS):
        part = pl.ds(i * rows, rows)
        loads.append(pltpu.make_async_copy(inverse_ref.at[0, part], inv_ref.at[part], load_sem.at[i]))
        loads[-1].start()
    onward, back = neighbours(size, 1), neighbours(size, -1)
    barrier = pltpu.get_barrier_semaphore()
    for device in onward + back:
        pl.semaphore_signal(barrier, inc=1, device_id=device, device_id_type=MESH)

    volume = 1.0 / NCELL
    partition, inside = cell_weights()
    kappa, face = permeability(labels_ref, perm_ref, inside)
    half = [f * (0.5 * volume) for f in face]
    weights = [jnp.concatenate([h * (p + ahead(p, s)) for h, s in zip(half, STRIDES)], axis=1).astype(bf)
               for p in partition]
    probe_rows = split3(probe_ref[...].T)

    total = None
    for i in range(CHUNKS):
        part = pl.ds(i * rows, rows)
        loads[i].wait()
        term = jnp.dot(sources_ref[0, :, part], inv_ref[part, :], preferred_element_type=f32)
        total = term if total is None else total + term
    snap_ref[...] = total.astype(bf)
    for r in range(0, SNAP, 64):
        field = snap_ref[r:r + 64, :].astype(f32)
        for d, stride in enumerate(STRIDES):
            grad_ref[r:r + 64, d * NCELL:(d + 1) * NCELL] = (ahead(field, stride) - field).astype(bf)

    def gram(corner):
        return lax.dot_general(grad_ref[...] * weights[corner], grad_ref[...], NT, preferred_element_type=f32)

    def triangle(g):
        return g[:128, :128], g[128:, :128], g[128:, 128:]

    probed = jnp.dot(probe_rows, snap_ref[...], preferred_element_type=f32)
    probed = probed[0:8] + probed[8:16] + probed[16:24]
    heavy = kappa * volume
    loads_ = jnp.concatenate([probed * (heavy * p) for p in partition], axis=0)
    side = lax.dot_general(split3(loads_), snap_ref[...], NT, preferred_element_type=f32)
    side = side[0:32] + side[32:64] + side[64:96]
    side = [side[8 * c:8 * c + 8] for c in range(4)]

    copies = []
    for slot, corner in ((2, 3), (1, 2), (0, 1)):
        for i, block in enumerate(triangle(gram(corner))):
            out_ref[slot, 128 * i:128 * i + 128, :] = block.astype(bf)
        hi = side[corner].astype(bf).astype(f32)
        low = side[corner] - hi
        out_ref[slot, 384:416, :] = jnp.concatenate(
            [hi[:, :128], hi[:, 128:], low[:, :128], low[:, 128:]], axis=0).astype(bf)
        copies.append(pltpu.make_async_remote_copy(
            src_ref=out_ref.at[slot], dst_ref=in_ref.at[slot], send_sem=send_sem.at[slot],
            recv_sem=recv_sem.at[slot], device_id=onward[slot], device_id_type=MESH))
        if slot == 2:
            pl.semaphore_wait(barrier, 6)
        copies[-1].start()

    own = list(triangle(gram(0)))
    own_side = side[0]
    for slot, copy in zip((2, 1, 0), copies):
        copy.wait_recv()
        for i in range(3):
            own[i] = own[i] + in_ref[slot, 128 * i:128 * i + 128, :].astype(f32)
        t = in_ref[slot, 384:416, :].astype(f32)
        own_side = own_side + jnp.concatenate([t[0:8] + t[16:24], t[8:16] + t[24:32]], axis=1)
    stiff_ref[:128, :128] = own[0]
    stiff_ref[128:, :128] = own[1]
    stiff_ref[:128, 128:] = own[1].T
    stiff_ref[128:, 128:] = own[2]
    side_ref[...] = own_side
    for copy in copies:
        copy.wait_send()


def front(size, labels, perm, inverse, sources, probe):
    return pl.pallas_call(
        functools.partial(front_kernel, size),
        out_shape=(jax.ShapeDtypeStruct((SNAP, NCELL), bf), jax.ShapeDtypeStruct((SNAP, SNAP), f32),
                   jax.ShapeDtypeStruct((NBASIS, SNAP), f32)),
        in_specs=[VMEM, pl.BlockSpec(memory_space=pltpu.SMEM), pl.BlockSpec(memory_space=pl.ANY), VMEM, VMEM],
        out_specs=(VMEM, VMEM, VMEM),
        scratch_shapes=[
            pltpu.VMEM((NCELL, NCELL), bf),
            pltpu.VMEM((SNAP, 3 * NCELL), bf),
            pltpu.VMEM((3, PACK, 128), bf),
            pltpu.VMEM((3, PACK, 128), bf),
            pltpu.SemaphoreType.DMA((CHUNKS,)),
            pltpu.SemaphoreType.DMA((3,)),
            pltpu.SemaphoreType.DMA((3,)),
        ],
        compiler_params=pltpu.CompilerParams(collective_id=0, has_side_effects=True),
        name="front",
    )(labels, perm, inverse, sources, probe)


def tail_kernel(size, labels_ref, perm_ref, snap_ref, coef_ref, element_ref, held_ref, send_ref, send_sem, recv_sem):
    onward, back = neighbours(size, 1), neighbours(size, -1)
    barrier = pltpu.get_barrier_semaphore()
    for device in onward + back:
        pl.semaphore_signal(barrier, inc=1, device_id=device, device_id_type=MESH)
    own = coef_ref[...].T.astype(bf).astype(f32)
    send_ref[...] = own
    pl.semaphore_wait(barrier, 6)
    copies = []
    for slot in (2, 1, 0):
        copies.append(pltpu.make_async_remote_copy(
            src_ref=send_ref, dst_ref=held_ref.at[slot], send_sem=send_sem.at[slot],
            recv_sem=recv_sem.at[slot], device_id=back[slot], device_id_type=MESH))
        copies[-1].start()
    partition, inside = cell_weights()
    kappa, face = permeability(labels_ref, perm_ref, inside)
    for copy in copies:
        copy.wait_recv()
    corners = jnp.concatenate([own, held_ref[0], held_ref[1], held_ref[2]], axis=0).astype(bf)
    field = jnp.dot(corners, snap_ref[...], preferred_element_type=f32)
    field = jnp.concatenate([field[8 * c:8 * c + 8] * partition[c] for c in range(4)], axis=0)
    slopes = [ahead(field, stride) - field for stride in STRIDES]
    left = jnp.concatenate([s * f for s, f in zip(slopes, face)], axis=1)
    right = jnp.concatenate(slopes, axis=1)
    element = lax.dot_general(left, right, NT, precision=HI, preferred_element_type=f32)
    element_ref[0] = element * (1.0 / (NCELL * SNAP))
    for copy in copies:
        copy.wait_send()


def tail(size, labels, perm, snap, coef):
    return pl.pallas_call(
        functools.partial(tail_kernel, size),
        out_shape=jax.ShapeDtypeStruct((1, 32, 32), f32),
        in_specs=[VMEM, pl.BlockSpec(memory_space=pltpu.SMEM), VMEM, VMEM],
        out_specs=VMEM,
        scratch_shapes=[
            pltpu.VMEM((3, NBASIS, SNAP), f32),
            pltpu.VMEM((NBASIS, SNAP), f32),
            pltpu.SemaphoreType.DMA((3,)),
            pltpu.SemaphoreType.DMA((3,)),
        ],
        compiler_params=pltpu.CompilerParams(collective_id=1, has_side_effects=True),
        name="tail",
    )(labels, perm, snap, coef)


def local(size, phase_labels, phase_perm, local_inverse, sources, shift, probe):
    snap, stiff, side = front(size, phase_labels, phase_perm, local_inverse, sources, probe)
    coefficients = solve(stiff, shift, side)
    element_stiffness = tail(size, phase_labels, phase_perm, snap, coefficients[0])
    return (coefficients, element_stiffness)


def solution(mesh):
    size = (mesh.shape["grp"], mesh.shape["sub"])
    in_specs = (
        P(("grp", "sub"), None),
        P(),
        P(("grp", "sub"), None, None),
        P(("grp", "sub"), None, None),
        P(("grp", "sub"), None),
        P(),
    )
    out_specs = (P(("grp", "sub"), None, None), P(("grp", "sub"), None, None))
    return jax.shard_map(functools.partial(local, size), mesh=mesh, in_specs=in_specs, out_specs=out_specs, check_vma=False)
```

```python
import functools
import jax
import jax.numpy as jnp
from jax import lax
from jax.experimental import pallas as pl
from jax.experimental.pallas import tpu as pltpu
from jax.sharding import PartitionSpec as P

HI = lax.Precision.HIGHEST
N = 256
NB = 16
W = 384
bf, f32 = jnp.bfloat16, jnp.float32


def spread(group, row):
    return jnp.broadcast_to(group[row:row + 1], (8, 128))


def leaf(cols, slabs):
    row = lax.broadcasted_iota(jnp.int32, (8, 128), 0)
    cols, slabs = list(cols), list(slabs)
    for p in range(0, NB, 2):
        g, i = p // 8, p % 8
        c0, c1 = cols[p], cols[p + 1]
        a, b = spread(c0[g], i), spread(c1[g], i)
        bt, d = spread(c0[g], i + 1), spread(c1[g], i + 1)
        inv = 1.0 / (a * d - b * bt)
        a, b, bt, d = a * inv, b * inv, bt * inv, d * inv
        e0 = [x * d - y * bt for x, y in zip(c0, c1)]
        e1 = [y * a - x * b for x, y in zip(c0, c1)]
        first, second = row == i, row == i + 1
        e0[g] = jnp.where(first, -d, jnp.where(second, bt, e0[g]))
        e1[g] = jnp.where(first, b, jnp.where(second, -a, e1[g]))
        pair = (row == i) | (row == i + 1)

        def step(t):
            r0, r1 = spread(t[g], i), spread(t[g], i + 1)
            z = list(t)
            z[g] = jnp.where(pair, 0.0, t[g])
            return [x - u * r0 - v * r1 for x, u, v in zip(z, e0, e1)]

        for q in range(p + 2, NB):
            cols[q] = step(cols[q])
        slabs = [step(t) for t in slabs]
    return slabs


def halves(x):
    hi = x.astype(bf)
    return hi, (x - hi.astype(f32)).astype(bf)


def column(tile, off, q):
    return [jnp.broadcast_to(t[:, off + q:off + q + 1], (8, 128)) for t in tile]


def eliminate(m_ref):
    steps = N // NB
    tile = lambda k: (k * NB) // 128

    def read(k, t):
        return [m_ref[k * NB + 8 * g:k * NB + 8 * g + 8, 128 * t:128 * t + 128] for g in range(2)]

    slab = {t: read(0, t) for t in range(3)}
    for k in range(steps):
        t0, off = tile(k), (k * NB) % 128
        cols = [column(slab[t0], off, q) for q in range(NB)]
        live = [t for t in range(3) if t == 2 or (t >= tile(k + 1) and k + 1 < steps)]
        new = dict(zip(live, leaf(cols, [slab[t] for t in live])))
        if k + 1 < steps:
            factor_tile = read(k + 1, t0)
            factors = [column(factor_tile, off, q) for q in range(NB)]
            nxt = {}
            for t in live:
                rows = [spread(new[t][q // 8], q % 8) for q in range(NB)]
                groups = []
                for g, start in enumerate(read(k + 1, t)):
                    parts = []
                    for c in range(0, NB, 4):
                        s = factors[c][g] * rows[c]
                        for q in range(c + 1, c + 4):
                            s = s + factors[q][g] * rows[q]
                        parts.append(s)
                    groups.append(start - ((parts[0] + parts[1]) + (parts[2] + parts[3])))
                nxt[t] = groups
        wide = jnp.concatenate([jnp.concatenate(new[t], axis=0) for t in live], axis=1)
        hi, low = halves(wide)
        width = 128 * len(live)
        gap = lambda n: [jnp.zeros((n, width), bf)] if n else []
        right = jnp.concatenate(
            [piece for x in (hi, hi, low, low) for piece in gap(off) + [x] + gap(128 - off - NB)], axis=0)
        lo = live[0] * 128

        def update(r0, r1):
            if r1 <= r0:
                return
            lhi, llow = halves(m_ref[r0:r1, 128 * t0:128 * t0 + 128])
            left = jnp.concatenate([lhi, llow, lhi, llow], axis=1)
            m_ref[r0:r1, lo:] = m_ref[r0:r1, lo:] - jnp.dot(left, right, preferred_element_type=f32)

        update((k + 2) * NB, N)
        update(0, k * NB)
        m_ref[k * NB:(k + 1) * NB, lo:] = wide
        if k + 1 < steps:
            slab = nxt


CELLX, CELLY, CELLZ, SNAP, NBASIS, PHASES, NCELL = 12, 12, 8, 256, 8, 3, 1152
STRIDES = (CELLY * CELLZ, CELLZ, 1)
CHUNKS = 3
PACK = 304
MESH = pl.DeviceIdType.MESH
NT = (((1,), (1,)), ((), ()))
VMEM = pl.BlockSpec(memory_space=pltpu.VMEM)


def ahead(field, stride):
    return pltpu.roll(field, NCELL - stride, axis=1)


def cell_weights():
    cell = lax.broadcasted_iota(jnp.int32, (1, NCELL), 1)
    run = lax.shift_right_logical(cell, 3)
    coord_x = lax.shift_right_logical(run * 683, 13)
    coord_y = run - coord_x * CELLY
    coord_z = lax.bitwise_and(cell, CELLZ - 1)
    fx = (coord_x.astype(f32) + 0.5) * (1.0 / CELLX)
    fy = (coord_y.astype(f32) + 0.5) * (1.0 / CELLY)
    partition = [(1.0 - fx) * (1.0 - fy), fx * (1.0 - fy), (1.0 - fx) * fy, fx * fy]
    inside = [coord_x < CELLX - 1, coord_y < CELLY - 1, coord_z < CELLZ - 1]
    return partition, inside


def permeability(labels_ref, perm_ref, inside):
    labels = labels_ref[...]
    kappa = jnp.where(labels == 0, perm_ref[0], jnp.where(labels == 1, perm_ref[1], perm_ref[2]))
    face = []
    for stride, keep in zip(STRIDES, inside):
        other = ahead(kappa, stride)
        face.append(jnp.where(keep, 2.0 * kappa * other / (kappa + other), 0.0))
    return kappa, face


def split3(x):
    hi = x.astype(bf)
    rest = x - hi.astype(f32)
    mid = rest.astype(bf)
    low = (rest - mid.astype(f32)).astype(bf)
    return jnp.concatenate([hi, mid, low], axis=0)


def neighbours(axes_size, step):
    grps, subs = axes_size
    g, s = lax.axis_index("grp"), lax.axis_index("sub")
    g1 = lax.rem(g + grps + step, grps)
    s1 = lax.rem(s + subs + step, subs)
    return [(g, s1), (g1, s), (g1, s1)]


def basis_kernel(size, labels_ref, perm_ref, inverse_ref, sources_ref, shift_ref, probe_ref,
                 coef_ref, element_ref, inv_ref, src_ref, snap_ref, grad_ref, out_ref, in_ref, m_ref,
                 coef_out_ref, coef_in_ref, load_sem, send_sem, recv_sem, coef_send_sem, coef_recv_sem):
    rows = NCELL // CHUNKS
    loads = []
    for i in range(CHUNKS):
        part = pl.ds(i * rows, rows)
        loads.append((
            pltpu.make_async_copy(sources_ref.at[0, :, part], src_ref.at[:, part], load_sem.at[0, i]),
            pltpu.make_async_copy(inverse_ref.at[0, part], inv_ref.at[part], load_sem.at[1, i])))
        for load in loads[-1]:
            load.start()
    onward, back = neighbours(size, 1), neighbours(size, -1)
    barrier = pltpu.get_barrier_semaphore()
    for device in onward + back:
        pl.semaphore_signal(barrier, inc=1, device_id=device, device_id_type=MESH)

    volume = 1.0 / NCELL
    partition, inside = cell_weights()
    kappa, face = permeability(labels_ref, perm_ref, inside)
    half = [f * (0.5 * volume) for f in face]
    weights = [jnp.concatenate([h * (p + ahead(p, s)) for h, s in zip(half, STRIDES)], axis=1).astype(bf)
               for p in partition]
    probe_rows = split3(probe_ref[...])

    total = None
    for i in range(CHUNKS):
        part = pl.ds(i * rows, rows)
        for load in loads[i]:
            load.wait()
        term = jnp.dot(src_ref[:, part], inv_ref[part, :], preferred_element_type=f32)
        total = term if total is None else total + term
    snap_ref[...] = total.astype(bf)
    for r in range(0, SNAP, 64):
        field = snap_ref[r:r + 64, :].astype(f32)
        for d, stride in enumerate(STRIDES):
            grad_ref[r:r + 64, d * NCELL:(d + 1) * NCELL] = (ahead(field, stride) - field).astype(bf)

    row = lax.broadcasted_iota(jnp.int32, (128, 128), 0)
    col = lax.broadcasted_iota(jnp.int32, (128, 128), 1)

    def gram(corner):
        g = lax.dot_general(grad_ref[...] * weights[corner], grad_ref[...], NT, preferred_element_type=f32)
        first, below, second = g[:128, :128], g[128:, :128], g[128:, 128:]
        diagonal = jnp.sum(jnp.where(row == col, second, 0.0), axis=0, keepdims=True)
        return [jnp.where(row >= col, first, second), below, diagonal]

    probed = jnp.dot(probe_rows, snap_ref[...], preferred_element_type=f32)
    probed = probed[0:8] + probed[8:16] + probed[16:24]
    heavy = kappa * volume
    loaded = jnp.concatenate([probed * (heavy * p) for p in partition], axis=0)
    side = lax.dot_general(split3(loaded), snap_ref[...], NT, preferred_element_type=f32)
    side = side[0:32] + side[32:64] + side[64:96]
    side = [side[8 * c:8 * c + 8] for c in range(4)]

    copies = {}
    for slot, corner in ((2, 3), (1, 2), (0, 1)):
        square, below, diagonal = gram(corner)
        hi = side[corner].astype(bf).astype(f32)
        low = side[corner] - hi
        out_ref[slot, 0:128, :] = square.astype(bf)
        out_ref[slot, 128:256, :] = below.astype(bf)
        out_ref[slot, 256:288, :] = jnp.concatenate(
            [hi[:, :128], hi[:, 128:], low[:, :128], low[:, 128:]], axis=0).astype(bf)
        out_ref[slot, 288:304, :] = jnp.broadcast_to(diagonal, (16, 128)).astype(bf)
        copies[slot] = pltpu.make_async_remote_copy(
            src_ref=out_ref.at[slot], dst_ref=in_ref.at[slot], send_sem=send_sem.at[slot],
            recv_sem=recv_sem.at[slot], device_id=onward[slot], device_id_type=MESH)
        if slot == 2:
            pl.semaphore_wait(barrier, 6)
        copies[slot].start()

    square, below, diagonal = gram(0)
    own_side = side[0]
    for slot in (0, 1, 2):
        copies[slot].wait_recv()
        square = square + in_ref[slot, 0:128, :].astype(f32)
        below = below + in_ref[slot, 128:256, :].astype(f32)
        t = in_ref[slot, 256:288, :].astype(f32)
        own_side = own_side + jnp.concatenate([t[0:8] + t[16:24], t[8:16] + t[24:32]], axis=1)
        diagonal = diagonal + in_ref[slot, 288:304, :].astype(f32)[0:1]
    turned = square.T
    shift = shift_ref[...]
    m_ref[:128, :128] = jnp.where(row >= col, square, turned) + jnp.where(row == col, shift[:, :128], 0.0)
    m_ref[128:, :128] = below
    m_ref[:128, 128:256] = below.T
    m_ref[128:, 128:256] = jnp.where(
        row == col, diagonal + shift[:, 128:], jnp.where(row < col, square, turned))
    m_ref[:, N:] = jnp.concatenate([own_side, jnp.zeros((120, SNAP), f32)], axis=0).T
    eliminate(m_ref)

    solved = m_ref[:, N:].T[0:8]
    coef_ref[0] = solved
    own = solved.astype(bf).astype(f32)
    coef_out_ref[...] = own
    sends = []
    for slot in (2, 1, 0):
        sends.append(pltpu.make_async_remote_copy(
            src_ref=coef_out_ref, dst_ref=coef_in_ref.at[slot], send_sem=coef_send_sem.at[slot],
            recv_sem=coef_recv_sem.at[slot], device_id=back[slot], device_id_type=MESH))
        sends[-1].start()
    for send in sends:
        send.wait_recv()
    corners = jnp.concatenate([own, coef_in_ref[0], coef_in_ref[1], coef_in_ref[2]], axis=0).astype(bf)
    field = jnp.dot(corners, snap_ref[...], preferred_element_type=f32)
    field = jnp.concatenate([field[8 * c:8 * c + 8] * partition[c] for c in range(4)], axis=0)
    slopes = [ahead(field, stride) - field for stride in STRIDES]
    left = jnp.concatenate([s * f for s, f in zip(slopes, face)], axis=1)
    right = jnp.concatenate(slopes, axis=1)
    element_ref[0] = lax.dot_general(left, right, NT, precision=HI, preferred_element_type=f32)
    for slot in copies:
        copies[slot].wait_send()
    for send in sends:
        send.wait_send()


def scale_kernel(coef_ref, element_ref, coef_out_ref, element_out_ref):
    coef_out_ref[...] = coef_ref[...]
    element_out_ref[...] = element_ref[...] * (1.0 / (NCELL * SNAP))


def local(size, phase_labels, phase_perm, local_inverse, sources, shift, probe):
    shapes = (jax.ShapeDtypeStruct((1, NBASIS, SNAP), f32), jax.ShapeDtypeStruct((1, 32, 32), f32))
    coef, element = pl.pallas_call(
        functools.partial(basis_kernel, size),
        out_shape=shapes,
        in_specs=[VMEM, pl.BlockSpec(memory_space=pltpu.SMEM), pl.BlockSpec(memory_space=pl.ANY),
                  pl.BlockSpec(memory_space=pl.ANY), VMEM, VMEM],
        out_specs=(VMEM, VMEM),
        scratch_shapes=[
            pltpu.VMEM((NCELL, NCELL), bf),
            pltpu.VMEM((SNAP, NCELL), bf),
            pltpu.VMEM((SNAP, NCELL), bf),
            pltpu.VMEM((SNAP, 3 * NCELL), bf),
            pltpu.VMEM((3, PACK, 128), bf),
            pltpu.VMEM((3, PACK, 128), bf),
            pltpu.VMEM((N, W), f32),
            pltpu.VMEM((NBASIS, SNAP), f32),
            pltpu.VMEM((3, NBASIS, SNAP), f32),
            pltpu.SemaphoreType.DMA((2, CHUNKS)),
            pltpu.SemaphoreType.DMA((3,)),
            pltpu.SemaphoreType.DMA((3,)),
            pltpu.SemaphoreType.DMA((3,)),
            pltpu.SemaphoreType.DMA((3,)),
        ],
        compiler_params=pltpu.CompilerParams(collective_id=0, has_side_effects=True),
        name="basis",
    )(phase_labels, phase_perm, local_inverse, sources, shift, probe.T)
    coef, element = pl.pallas_call(
        scale_kernel, out_shape=shapes, in_specs=[VMEM, VMEM], out_specs=(VMEM, VMEM), name="scale",
    )(coef, element)
    return (coef.transpose(0, 2, 1), element)


def solution(mesh):
    size = (mesh.shape["grp"], mesh.shape["sub"])
    in_specs = (
        P(("grp", "sub"), None),
        P(),
        P(("grp", "sub"), None, None),
        P(("grp", "sub"), None, None),
        P(("grp", "sub"), None),
        P(),
    )
    out_specs = (P(("grp", "sub"), None, None), P(("grp", "sub"), None, None))
    return jax.shard_map(functools.partial(local, size), mesh=mesh, in_specs=in_specs, out_specs=out_specs, check_vma=False)
```

```python
import functools
import jax
import jax.numpy as jnp
from jax import lax
from jax.experimental import pallas as pl
from jax.experimental.pallas import tpu as pltpu
from jax.sharding import PartitionSpec as P

HI = lax.Precision.HIGHEST
N = 256
NB = 16
W = 384
NBASIS = 8
bf, f32 = jnp.bfloat16, jnp.float32


def spread(group, row):
    return jnp.broadcast_to(group[row:row + 1], (8, 128))


def leaf(cols, slabs):
    row = lax.broadcasted_iota(jnp.int32, (8, 128), 0)
    cols, slabs = list(cols), list(slabs)
    for p in range(0, NB, 2):
        g, i = p // 8, p % 8
        c0, c1 = cols[p], cols[p + 1]
        a, b = spread(c0[g], i), spread(c1[g], i)
        bt, d = spread(c0[g], i + 1), spread(c1[g], i + 1)
        inv = 1.0 / (a * d - b * bt)
        a, b, bt, d = a * inv, b * inv, bt * inv, d * inv
        e0 = [x * d - y * bt for x, y in zip(c0, c1)]
        e1 = [y * a - x * b for x, y in zip(c0, c1)]
        first, second = row == i, row == i + 1
        e0[g] = jnp.where(first, -d, jnp.where(second, bt, e0[g]))
        e1[g] = jnp.where(first, b, jnp.where(second, -a, e1[g]))
        pair = (row == i) | (row == i + 1)

        def step(t):
            r0, r1 = spread(t[g], i), spread(t[g], i + 1)
            z = list(t)
            z[g] = jnp.where(pair, 0.0, t[g])
            return [x - u * r0 - v * r1 for x, u, v in zip(z, e0, e1)]

        for q in range(p + 2, NB):
            cols[q] = step(cols[q])
        slabs = [step(t) for t in slabs]
    return slabs


def halves(x):
    hi = x.astype(bf)
    return hi, (x - hi.astype(f32)).astype(bf)


def column(tile, off, q):
    return [jnp.broadcast_to(t[:, off + q:off + q + 1], (8, 128)) for t in tile]


def eliminate(m_ref):
    steps = N // NB
    tile = lambda k: (k * NB) // 128
    low8 = lambda rows: lax.broadcasted_iota(jnp.int32, (rows, 128), 1) < NBASIS

    def moved(k, pieces):
        if k == 0:
            return {0: jnp.where(low8(pieces[0].shape[0]), pieces[2], pieces[0]), 1: pieces[1]}
        if k == 8:
            return {1: jnp.where(low8(pieces[1].shape[0]), pieces[0], pieces[1])}
        return pieces

    def read(k, t):
        return [m_ref[k * NB + 8 * g:k * NB + 8 * g + 8, 128 * t:128 * t + 128] for g in range(2)]

    slab = {t: read(0, t) for t in range(3)}
    for k in range(steps):
        t0, off = tile(k), (k * NB) % 128
        cols = [column(slab[t0], off, q) for q in range(NB)]
        live = [0, 1, 2] if k == 0 else [0, 1] if k <= 8 else [1]
        new = dict(zip(live, leaf(cols, [slab[t] for t in live])))
        if k + 1 < steps:
            factor_tile = read(k + 1, t0)
            factors = [column(factor_tile, off, q) for q in range(NB)]
            nxt = {}
            for t in live:
                rows = [spread(new[t][q // 8], q % 8) for q in range(NB)]
                groups = []
                for g, start in enumerate(read(k + 1, t)):
                    parts = []
                    for c in range(0, NB, 4):
                        s = factors[c][g] * rows[c]
                        for q in range(c + 1, c + 4):
                            s = s + factors[q][g] * rows[q]
                        parts.append(s)
                    groups.append(start - ((parts[0] + parts[1]) + (parts[2] + parts[3])))
                nxt[t] = groups
            both = [moved(k, {t: nxt[t][g] for t in live}) for g in range(2)]
            slab = {t: [both[0][t], both[1][t]] for t in both[0]}
        new = {t: jnp.concatenate(new[t], axis=0) for t in live}
        hi, low = halves(jnp.concatenate([new[t] for t in live], axis=1))
        width = 128 * len(live)
        gap = lambda n: [jnp.zeros((n, width), bf)] if n else []
        right = jnp.concatenate(
            [piece for x in (hi, hi, low, low) for piece in gap(off) + [x] + gap(128 - off - NB)], axis=0)
        lo = live[0] * 128

        def update(r0, r1):
            if r1 <= r0:
                return
            lhi, llow = halves(m_ref[r0:r1, 128 * t0:128 * t0 + 128])
            left = jnp.concatenate([lhi, llow, lhi, llow], axis=1)
            got = m_ref[r0:r1, lo:lo + width] - jnp.dot(left, right, preferred_element_type=f32)
            pieces = moved(k, {t: got[:, 128 * i:128 * i + 128] for i, t in enumerate(live)})
            for t in pieces:
                m_ref[r0:r1, 128 * t:128 * t + 128] = pieces[t]

        update((k + 2) * NB, N)
        update(0, k * NB)
        pieces = moved(k, new)
        for t in pieces:
            m_ref[k * NB:(k + 1) * NB, 128 * t:128 * t + 128] = pieces[t]


CELLX, CELLY, CELLZ, SNAP, NBASIS, PHASES, NCELL = 12, 12, 8, 256, 8, 3, 1152
STRIDES = (CELLY * CELLZ, CELLZ, 1)
CHUNKS = ((0, 256), (256, 768), (768, 1152))
PACK = 272
MESH = pl.DeviceIdType.MESH
NT = (((1,), (1,)), ((), ()))
VMEM = pl.BlockSpec(memory_space=pltpu.VMEM)


def ahead(field, stride):
    return pltpu.roll(field, NCELL - stride, axis=1)


def cell_weights():
    cell = lax.broadcasted_iota(jnp.int32, (1, NCELL), 1)
    run = lax.shift_right_logical(cell, 3)
    coord_x = lax.shift_right_logical(run * 683, 13)
    coord_y = run - coord_x * CELLY
    coord_z = lax.bitwise_and(cell, CELLZ - 1)
    fx = (coord_x.astype(f32) + 0.5) * (1.0 / CELLX)
    fy = (coord_y.astype(f32) + 0.5) * (1.0 / CELLY)
    partition = [(1.0 - fx) * (1.0 - fy), fx * (1.0 - fy), (1.0 - fx) * fy, fx * fy]
    inside = [coord_x < CELLX - 1, coord_y < CELLY - 1, coord_z < CELLZ - 1]
    return partition, inside


def permeability(labels_ref, perm_ref, inside):
    labels, perm = labels_ref[...], perm_ref[...]
    kappa = jnp.where(labels == 0, perm[:, 0:1], jnp.where(labels == 1, perm[:, 1:2], perm[:, 2:3]))
    face = []
    for stride, keep in zip(STRIDES, inside):
        other = ahead(kappa, stride)
        face.append(jnp.where(keep, 2.0 * kappa * other / (kappa + other), 0.0))
    return kappa, face


def split3(x):
    hi = x.astype(bf)
    rest = x - hi.astype(f32)
    mid = rest.astype(bf)
    low = (rest - mid.astype(f32)).astype(bf)
    return jnp.concatenate([hi, mid, low], axis=0)


def neighbours(axes_size, step):
    grps, subs = axes_size
    g, s = lax.axis_index("grp"), lax.axis_index("sub")
    g1 = lax.rem(g + grps + step, grps)
    s1 = lax.rem(s + subs + step, subs)
    return [(g, s1), (g1, s), (g1, s1)]


def basis_kernel(size, labels_hbm, perm_hbm, inverse_ref, sources_ref, shift_hbm, probe_hbm,
                 coef_ref, element_ref, labels_ref, perm_ref, shift_ref, probe_ref, inv_ref, src_ref, snap_ref,
                 grad_ref, out_ref, in_ref, side_out_ref, side_in_ref, m_ref, coef_out_ref, coef_in_ref,
                 small_sem, load_sem, send_sem, recv_sem, side_send_sem, side_recv_sem, coef_send_sem, coef_recv_sem):
    onward, back = neighbours(size, 1), neighbours(size, -1)
    loads = [pltpu.make_async_copy(sources_ref.at[0], src_ref, load_sem.at[0])]
    for i, (start, stop) in enumerate(CHUNKS):
        part = pl.ds(start, stop - start)
        loads.append(pltpu.make_async_copy(inverse_ref.at[0, :, part], inv_ref.at[:, part], load_sem.at[i + 1]))
    small = [pltpu.make_async_copy(source, target, small_sem.at[i]) for i, (source, target) in enumerate(
        ((labels_hbm, labels_ref), (perm_hbm, perm_ref), (shift_hbm, shift_ref), (probe_hbm, probe_ref)))]
    for load in loads[:2] + small + loads[2:]:
        load.start()
    barrier = pltpu.get_barrier_semaphore()
    for device in onward + back:
        pl.semaphore_signal(barrier, inc=1, device_id=device, device_id_type=MESH)

    volume = 1.0 / NCELL
    partition, inside = cell_weights()
    for load in small:
        load.wait()
    kappa, face = permeability(labels_ref, perm_ref, inside)
    half = [f * (0.5 * volume) for f in face]
    weights = [jnp.concatenate([h * (p + ahead(p, s)) for h, s in zip(half, STRIDES)], axis=1).astype(bf)
               for p in partition]
    probe_rows = split3(probe_ref[...])

    loads[0].wait()
    for i, (start, stop) in enumerate(CHUNKS):
        loads[i + 1].wait()
        snap_ref[:, start:stop] = jnp.dot(
            src_ref[...], inv_ref[:, start:stop], preferred_element_type=f32).astype(bf)
    for r in range(0, SNAP, 64):
        field = snap_ref[r:r + 64, :].astype(f32)
        for d, stride in enumerate(STRIDES):
            grad_ref[r:r + 64, d * NCELL:(d + 1) * NCELL] = (ahead(field, stride) - field).astype(bf)

    row = lax.broadcasted_iota(jnp.int32, (128, 128), 0)
    col = lax.broadcasted_iota(jnp.int32, (128, 128), 1)

    def gram(corner):
        g = lax.dot_general(grad_ref[...] * weights[corner], grad_ref[...], NT, preferred_element_type=f32)
        first, below, second = g[:128, :128], g[128:, :128], g[128:, 128:]
        diagonal = jnp.sum(jnp.where(row == col, second, 0.0), axis=0, keepdims=True)
        return [jnp.where(row >= col, first, second), below, diagonal]

    def remote(sources, targets, slot, send, recv, device):
        return pltpu.make_async_remote_copy(
            src_ref=sources, dst_ref=targets.at[slot], send_sem=send.at[slot], recv_sem=recv.at[slot],
            device_id=device, device_id_type=MESH)

    def pack(slot, square, below, diagonal):
        out_ref[slot, 0:128, :] = square.astype(bf)
        out_ref[slot, 128:256, :] = below.astype(bf)
        out_ref[slot, 256:272, :] = jnp.broadcast_to(diagonal, (16, 128)).astype(bf)

    def plus(slot, square, below, diagonal):
        return (square + in_ref[slot, 0:128, :].astype(f32), below + in_ref[slot, 128:256, :].astype(f32),
                diagonal + in_ref[slot, 256:272, :].astype(f32)[0:1])

    across = {slot: remote(out_ref.at[slot], in_ref, slot, send_sem, recv_sem, device)
              for slot, device in ((2, onward[0]), (0, onward[0]), (1, onward[1]))}
    pack(2, *gram(3))
    pl.semaphore_wait(barrier, 6)
    across[2].start()
    upper = gram(2)
    pack(0, *gram(1))
    across[0].start()

    probed = jnp.dot(probe_rows, snap_ref[...], preferred_element_type=f32)
    probed = probed[0:8] + probed[8:16] + probed[16:24]
    heavy = kappa * volume
    loaded = jnp.concatenate([probed * (heavy * p) for p in partition], axis=0)
    side = lax.dot_general(split3(loaded), snap_ref[...], NT, preferred_element_type=f32)
    side = side[0:32] + side[32:64] + side[64:96]
    side_out_ref[...] = side
    sides = []
    for slot in (2, 1, 0):
        corner = slot + 1
        sides.append(remote(side_out_ref.at[pl.ds(8 * corner, 8)], side_in_ref, slot, side_send_sem, side_recv_sem,
                            onward[slot]))
        sides[-1].start()

    across[2].wait_recv()
    pack(1, *plus(2, *upper))
    across[1].start()
    own = gram(0)
    own_side = side[0:8]
    for copy in sides:
        copy.wait_recv()
    own_side = own_side + (side_in_ref[0] + side_in_ref[1] + side_in_ref[2])
    across[0].wait_recv()
    own = plus(0, *own)
    across[1].wait_recv()
    square, below, diagonal = plus(1, *own)
    turned = square.T
    shift = shift_ref[...]
    m_ref[:128, :128] = jnp.where(row >= col, square, turned) + jnp.where(row == col, shift[:, :128], 0.0)
    m_ref[128:, :128] = below
    m_ref[:128, 128:256] = below.T
    m_ref[128:, 128:256] = jnp.where(
        row == col, diagonal + shift[:, 128:], jnp.where(row < col, square, turned))
    m_ref[:, N:] = jnp.concatenate([own_side, jnp.zeros((120, SNAP), f32)], axis=0).T
    eliminate(m_ref)

    solved = m_ref[:, 128:256].T[0:8]
    coef_ref[0] = solved
    own = solved.astype(bf).astype(f32)
    coef_out_ref[...] = own
    sends = []
    for slot in (2, 1, 0):
        sends.append(pltpu.make_async_remote_copy(
            src_ref=coef_out_ref, dst_ref=coef_in_ref.at[slot], send_sem=coef_send_sem.at[slot],
            recv_sem=coef_recv_sem.at[slot], device_id=back[slot], device_id_type=MESH))
        sends[-1].start()
    for send in sends:
        send.wait_recv()
    corners = jnp.concatenate([own, coef_in_ref[0], coef_in_ref[1], coef_in_ref[2]], axis=0).astype(bf)
    field = jnp.dot(corners, snap_ref[...], preferred_element_type=f32)
    field = jnp.concatenate([field[8 * c:8 * c + 8] * partition[c] for c in range(4)], axis=0)
    slopes = [ahead(field, stride) - field for stride in STRIDES]
    left = jnp.concatenate(halves(jnp.concatenate([s * f for s, f in zip(slopes, face)], axis=1)), axis=0)
    right = jnp.concatenate(halves(jnp.concatenate(slopes, axis=1)), axis=0)
    product = lax.dot_general(left, right, NT, preferred_element_type=f32)
    product = product[0:32] + product[32:64]
    element_ref[0] = product[:, 0:32] + product[:, 32:64]
    for copy in list(across.values()) + sides + sends:
        copy.wait_send()


def scale_kernel(coef_ref, element_ref, coef_out_ref, element_out_ref):
    coef_out_ref[...] = coef_ref[...]
    element_out_ref[...] = element_ref[...] * (1.0 / (NCELL * SNAP))


def local(size, phase_labels, phase_perm, local_inverse, sources, shift, probe):
    shapes = (jax.ShapeDtypeStruct((1, NBASIS, SNAP), f32), jax.ShapeDtypeStruct((1, 32, 32), f32))
    coef, element = pl.pallas_call(
        functools.partial(basis_kernel, size),
        out_shape=shapes,
        in_specs=[pl.BlockSpec(memory_space=pl.ANY)] * 6,
        out_specs=(VMEM, VMEM),
        scratch_shapes=[
            pltpu.VMEM((1, NCELL), jnp.int32),
            pltpu.VMEM((1, PHASES), f32),
            pltpu.VMEM((1, SNAP), f32),
            pltpu.VMEM((NBASIS, SNAP), f32),
            pltpu.VMEM((NCELL, NCELL), bf),
            pltpu.VMEM((SNAP, NCELL), bf),
            pltpu.VMEM((SNAP, NCELL), bf),
            pltpu.VMEM((SNAP, 3 * NCELL), bf),
            pltpu.VMEM((3, PACK, 128), bf),
            pltpu.VMEM((3, PACK, 128), bf),
            pltpu.VMEM((4 * NBASIS, SNAP), f32),
            pltpu.VMEM((3, NBASIS, SNAP), f32),
            pltpu.VMEM((N, W), f32),
            pltpu.VMEM((NBASIS, SNAP), f32),
            pltpu.VMEM((3, NBASIS, SNAP), f32),
            pltpu.SemaphoreType.DMA((4,)),
            pltpu.SemaphoreType.DMA((1 + len(CHUNKS),)),
            pltpu.SemaphoreType.DMA((3,)),
            pltpu.SemaphoreType.DMA((3,)),
            pltpu.SemaphoreType.DMA((3,)),
            pltpu.SemaphoreType.DMA((3,)),
            pltpu.SemaphoreType.DMA((3,)),
            pltpu.SemaphoreType.DMA((3,)),
        ],
        compiler_params=pltpu.CompilerParams(collective_id=0, has_side_effects=True),
        name="basis",
    )(phase_labels, phase_perm.reshape(1, PHASES), local_inverse, sources, shift, probe.T)
    coef, element = pl.pallas_call(
        scale_kernel, out_shape=shapes, in_specs=[VMEM, VMEM], out_specs=(VMEM, VMEM), name="scale",
    )(coef, element)
    return (coef.transpose(0, 2, 1), element)


def solution(mesh):
    size = (mesh.shape["grp"], mesh.shape["sub"])
    in_specs = (
        P(("grp", "sub"), None),
        P(),
        P(("grp", "sub"), None, None),
        P(("grp", "sub"), None, None),
        P(("grp", "sub"), None),
        P(),
    )
    out_specs = (P(("grp", "sub"), None, None), P(("grp", "sub"), None, None))
    return jax.shard_map(functools.partial(local, size), mesh=mesh, in_specs=in_specs, out_specs=out_specs, check_vma=False)
```

```python
import functools
import jax
import jax.numpy as jnp
from jax import lax
from jax.experimental import pallas as pl
from jax.experimental.pallas import tpu as pltpu
from jax.sharding import PartitionSpec as P

HI = lax.Precision.HIGHEST
N = 256
NB = 16
W = 384
NBASIS = 8
bf, f32 = jnp.bfloat16, jnp.float32


def spread(group, row):
    return jnp.broadcast_to(group[row:row + 1], (8, 128))


def leaf(cols, slabs):
    row = lax.broadcasted_iota(jnp.int32, (8, 128), 0)
    cols, slabs = list(cols), list(slabs)
    for p in range(0, NB, 2):
        g, i = p // 8, p % 8
        c0, c1 = cols[p], cols[p + 1]
        a, b = spread(c0[g], i), spread(c1[g], i)
        bt, d = spread(c0[g], i + 1), spread(c1[g], i + 1)
        inv = 1.0 / (a * d - b * bt)
        a, b, bt, d = a * inv, b * inv, bt * inv, d * inv
        e0 = [x * d - y * bt for x, y in zip(c0, c1)]
        e1 = [y * a - x * b for x, y in zip(c0, c1)]
        first, second = row == i, row == i + 1
        e0[g] = jnp.where(first, -d, jnp.where(second, bt, e0[g]))
        e1[g] = jnp.where(first, b, jnp.where(second, -a, e1[g]))
        pair = (row == i) | (row == i + 1)

        def step(t):
            r0, r1 = spread(t[g], i), spread(t[g], i + 1)
            z = list(t)
            z[g] = jnp.where(pair, 0.0, t[g])
            return [x - u * r0 - v * r1 for x, u, v in zip(z, e0, e1)]

        for q in range(p + 2, NB):
            cols[q] = step(cols[q])
        slabs = [step(t) for t in slabs]
    return slabs


def halves(x):
    hi = x.astype(bf)
    return hi, (x - hi.astype(f32)).astype(bf)


def column(tile, off, q):
    return [jnp.broadcast_to(t[:, off + q:off + q + 1], (8, 128)) for t in tile]


def eliminate(m_ref):
    steps = N // NB
    tile = lambda k: (k * NB) // 128
    low8 = lambda rows: lax.broadcasted_iota(jnp.int32, (rows, 128), 1) < NBASIS

    def moved(k, pieces):
        if k == 0:
            return {0: jnp.where(low8(pieces[0].shape[0]), pieces[2], pieces[0]), 1: pieces[1]}
        if k == 8:
            return {1: jnp.where(low8(pieces[1].shape[0]), pieces[0], pieces[1])}
        return pieces

    def read(k, t):
        return [m_ref[k * NB + 8 * g:k * NB + 8 * g + 8, 128 * t:128 * t + 128] for g in range(2)]

    slab = {t: read(0, t) for t in range(3)}
    for k in range(steps):
        t0, off = tile(k), (k * NB) % 128
        cols = [column(slab[t0], off, q) for q in range(NB)]
        live = [0, 1, 2] if k == 0 else [0, 1] if k <= 8 else [1]
        new = dict(zip(live, leaf(cols, [slab[t] for t in live])))
        if k + 1 < steps:
            factor_tile = read(k + 1, t0)
            factors = [column(factor_tile, off, q) for q in range(NB)]
            nxt = {}
            for t in live:
                rows = [spread(new[t][q // 8], q % 8) for q in range(NB)]
                groups = []
                for g, start in enumerate(read(k + 1, t)):
                    parts = []
                    for c in range(0, NB, 4):
                        s = factors[c][g] * rows[c]
                        for q in range(c + 1, c + 4):
                            s = s + factors[q][g] * rows[q]
                        parts.append(s)
                    groups.append(start - ((parts[0] + parts[1]) + (parts[2] + parts[3])))
                nxt[t] = groups
            both = [moved(k, {t: nxt[t][g] for t in live}) for g in range(2)]
            slab = {t: [both[0][t], both[1][t]] for t in both[0]}
        new = {t: jnp.concatenate(new[t], axis=0) for t in live}
        hi, low = halves(jnp.concatenate([new[t] for t in live], axis=1))
        width = 128 * len(live)
        gap = lambda n: [jnp.zeros((n, width), bf)] if n else []
        right = jnp.concatenate(
            [piece for x in (hi, hi, low, low) for piece in gap(off) + [x] + gap(128 - off - NB)], axis=0)
        lo = live[0] * 128

        def update(r0, r1):
            if r1 <= r0:
                return
            lhi, llow = halves(m_ref[r0:r1, 128 * t0:128 * t0 + 128])
            left = jnp.concatenate([lhi, llow, lhi, llow], axis=1)
            got = m_ref[r0:r1, lo:lo + width] - jnp.dot(left, right, preferred_element_type=f32)
            pieces = moved(k, {t: got[:, 128 * i:128 * i + 128] for i, t in enumerate(live)})
            for t in pieces:
                m_ref[r0:r1, 128 * t:128 * t + 128] = pieces[t]

        update((k + 2) * NB, N)
        update(0, k * NB)
        pieces = moved(k, new)
        for t in pieces:
            m_ref[k * NB:(k + 1) * NB, 128 * t:128 * t + 128] = pieces[t]


CELLX, CELLY, CELLZ, SNAP, NBASIS, PHASES, NCELL = 12, 12, 8, 256, 8, 3, 1152
STRIDES = (CELLY * CELLZ, CELLZ, 1)
CHUNKS = ((0, 256), (256, 768), (768, 1152))
PACK = 272
MESH = pl.DeviceIdType.MESH
NT = (((1,), (1,)), ((), ()))
VMEM = pl.BlockSpec(memory_space=pltpu.VMEM)


def ahead(field, stride):
    return pltpu.roll(field, NCELL - stride, axis=1)


def cell_weights():
    cell = lax.broadcasted_iota(jnp.int32, (1, NCELL), 1)
    run = lax.shift_right_logical(cell, 3)
    coord_x = lax.shift_right_logical(run * 683, 13)
    coord_y = run - coord_x * CELLY
    coord_z = lax.bitwise_and(cell, CELLZ - 1)
    fx = (coord_x.astype(f32) + 0.5) * (1.0 / CELLX)
    fy = (coord_y.astype(f32) + 0.5) * (1.0 / CELLY)
    partition = [(1.0 - fx) * (1.0 - fy), fx * (1.0 - fy), (1.0 - fx) * fy, fx * fy]
    inside = [coord_x < CELLX - 1, coord_y < CELLY - 1, coord_z < CELLZ - 1]
    return partition, inside


def permeability(labels_ref, perm_ref, inside):
    labels, perm = labels_ref[...], perm_ref[...]
    kappa = jnp.where(labels == 0, perm[:, 0:1], jnp.where(labels == 1, perm[:, 1:2], perm[:, 2:3]))
    face = []
    for stride, keep in zip(STRIDES, inside):
        other = ahead(kappa, stride)
        face.append(jnp.where(keep, 2.0 * kappa * other / (kappa + other), 0.0))
    return kappa, face


def split3(x):
    hi = x.astype(bf)
    rest = x - hi.astype(f32)
    mid = rest.astype(bf)
    low = (rest - mid.astype(f32)).astype(bf)
    return jnp.concatenate([hi, mid, low], axis=0)


def neighbours(axes_size, step):
    grps, subs = axes_size
    g, s = lax.axis_index("grp"), lax.axis_index("sub")
    g1 = lax.rem(g + grps + step, grps)
    s1 = lax.rem(s + subs + step, subs)
    return [(g, s1), (g1, s), (g1, s1)]


def basis_kernel(size, labels_hbm, perm_hbm, inverse_ref, sources_ref, shift_hbm, probe_hbm,
                 coef_ref, element_ref, labels_ref, perm_ref, shift_ref, probe_ref, inv_ref, src_ref, snap_ref,
                 grad_ref, out_ref, in_ref, side_out_ref, side_in_ref, m_ref, coef_out_ref, coef_in_ref,
                 small_sem, load_sem, send_sem, recv_sem, side_send_sem, side_recv_sem, coef_send_sem, coef_recv_sem):
    onward, back = neighbours(size, 1), neighbours(size, -1)
    loads = [pltpu.make_async_copy(sources_ref.at[0], src_ref, load_sem.at[0])]
    for i, (start, stop) in enumerate(CHUNKS):
        part = pl.ds(start, stop - start)
        loads.append(pltpu.make_async_copy(inverse_ref.at[0, :, part], inv_ref.at[:, part], load_sem.at[i + 1]))
    small = [pltpu.make_async_copy(source, target, small_sem.at[i]) for i, (source, target) in enumerate(
        ((labels_hbm, labels_ref), (perm_hbm, perm_ref), (shift_hbm, shift_ref), (probe_hbm, probe_ref)))]
    for load in loads[:2] + small + loads[2:]:
        load.start()
    barrier = pltpu.get_barrier_semaphore()
    for device in back:
        pl.semaphore_signal(barrier, inc=1, device_id=device, device_id_type=MESH)

    volume = 1.0 / NCELL
    partition, inside = cell_weights()
    for load in small:
        load.wait()
    kappa, face = permeability(labels_ref, perm_ref, inside)
    half = [f * (0.5 * volume) for f in face]
    weights = [jnp.concatenate([h * (p + ahead(p, s)) for h, s in zip(half, STRIDES)], axis=1).astype(bf)
               for p in partition]
    probe_rows = split3(probe_ref[...])

    loads[0].wait()
    for i, (start, stop) in enumerate(CHUNKS):
        loads[i + 1].wait()
        snap_ref[:, start:stop] = jnp.dot(
            src_ref[...], inv_ref[:, start:stop], preferred_element_type=f32).astype(bf)
    for r in range(0, SNAP, 64):
        field = snap_ref[r:r + 64, :]
        for d, stride in enumerate(STRIDES):
            grad_ref[r:r + 64, d * NCELL:(d + 1) * NCELL] = ahead(field, stride) - field

    row = lax.broadcasted_iota(jnp.int32, (128, 128), 0)
    col = lax.broadcasted_iota(jnp.int32, (128, 128), 1)

    def gram(corner):
        g = lax.dot_general(grad_ref[...] * weights[corner], grad_ref[...], NT, preferred_element_type=f32)
        first, below, second = g[:128, :128], g[128:, :128], g[128:, 128:]
        diagonal = jnp.sum(jnp.where(row == col, second, 0.0), axis=0, keepdims=True)
        return [jnp.where(row >= col, first, second), below, diagonal]

    def remote(sources, targets, slot, send, recv, device):
        return pltpu.make_async_remote_copy(
            src_ref=sources, dst_ref=targets.at[slot], send_sem=send.at[slot], recv_sem=recv.at[slot],
            device_id=device, device_id_type=MESH)

    def pack(slot, square, below, diagonal):
        out_ref[slot, 0:128, :] = square.astype(bf)
        out_ref[slot, 128:256, :] = below.astype(bf)
        out_ref[slot, 256:272, :] = jnp.broadcast_to(diagonal, (16, 128)).astype(bf)

    def plus(slot, square, below, diagonal):
        return (square + in_ref[slot, 0:128, :].astype(f32), below + in_ref[slot, 128:256, :].astype(f32),
                diagonal + in_ref[slot, 256:272, :].astype(f32)[0:1])

    across = [remote(out_ref.at[slot], in_ref, slot, send_sem, recv_sem, onward[slot]) for slot in range(3)]
    both = gram(3), gram(2)
    pack(2, *both[0])
    pack(1, *both[1])
    pl.semaphore_wait(barrier, 3)
    across[2].start()
    across[1].start()

    probed = jnp.dot(probe_rows, snap_ref[...], preferred_element_type=f32)
    probed = probed[0:8] + probed[8:16] + probed[16:24]
    heavy = kappa * volume
    loaded = jnp.concatenate([probed * (heavy * p) for p in partition], axis=0)
    side = lax.dot_general(split3(loaded), snap_ref[...], NT, preferred_element_type=f32)
    side = side[0:32] + side[32:64] + side[64:96]
    side_out_ref[...] = side
    sides = []
    for slot in (2, 1, 0):
        corner = slot + 1
        sides.append(remote(side_out_ref.at[pl.ds(8 * corner, 8)], side_in_ref, slot, side_send_sem, side_recv_sem,
                            onward[slot]))
        sides[-1].start()

    beside, own = gram(1), gram(0)
    pack(0, *beside)
    across[0].start()
    own_side = side[0:8]
    for copy in sides:
        copy.wait_recv()
    own_side = own_side + (side_in_ref[0] + side_in_ref[1] + side_in_ref[2])
    for slot in (0, 2, 1):
        across[slot].wait_recv()
        own = plus(slot, *own)
    square, below, diagonal = own
    turned = square.T
    shift = shift_ref[...]
    m_ref[:128, :128] = jnp.where(row >= col, square, turned) + jnp.where(row == col, shift[:, :128], 0.0)
    m_ref[128:, :128] = below
    m_ref[:128, 128:256] = below.T
    m_ref[128:, 128:256] = jnp.where(
        row == col, diagonal + shift[:, 128:], jnp.where(row < col, square, turned))
    m_ref[:, N:] = jnp.concatenate([own_side, jnp.zeros((120, SNAP), f32)], axis=0).T
    eliminate(m_ref)

    solved = m_ref[:, 128:256].T[0:8]
    coef_ref[0] = solved
    own = solved.astype(bf).astype(f32)
    coef_out_ref[...] = own
    sends = []
    for slot in (2, 1, 0):
        sends.append(pltpu.make_async_remote_copy(
            src_ref=coef_out_ref, dst_ref=coef_in_ref.at[slot], send_sem=coef_send_sem.at[slot],
            recv_sem=coef_recv_sem.at[slot], device_id=back[slot], device_id_type=MESH))
        sends[-1].start()
    for send in sends:
        send.wait_recv()
    corners = jnp.concatenate([own, coef_in_ref[0], coef_in_ref[1], coef_in_ref[2]], axis=0).astype(bf)
    field = jnp.dot(corners, snap_ref[...], preferred_element_type=f32)
    field = jnp.concatenate([field[8 * c:8 * c + 8] * partition[c] for c in range(4)], axis=0)
    slopes = [ahead(field, stride) - field for stride in STRIDES]
    left = jnp.concatenate(halves(jnp.concatenate([s * f for s, f in zip(slopes, face)], axis=1)), axis=0)
    right = jnp.concatenate(halves(jnp.concatenate(slopes, axis=1)), axis=0)
    product = (lax.dot_general(left[:, :1792], right[:, :1792], NT, preferred_element_type=f32)
               + lax.dot_general(left[:, 1792:], right[:, 1792:], NT, preferred_element_type=f32))
    product = product[0:32] + product[32:64]
    element_ref[0] = product[:, 0:32] + product[:, 32:64]
    for copy in across + sides + sends:
        copy.wait_send()


def scale_kernel(coef_ref, element_ref, coef_out_ref, element_out_ref):
    coef_out_ref[...] = coef_ref[...]
    element_out_ref[...] = element_ref[...] * (1.0 / (NCELL * SNAP))


def local(size, phase_labels, phase_perm, local_inverse, sources, shift, probe):
    shapes = (jax.ShapeDtypeStruct((1, NBASIS, SNAP), f32), jax.ShapeDtypeStruct((1, 32, 32), f32))
    coef, element = pl.pallas_call(
        functools.partial(basis_kernel, size),
        out_shape=shapes,
        in_specs=[pl.BlockSpec(memory_space=pl.ANY)] * 6,
        out_specs=(VMEM, VMEM),
        scratch_shapes=[
            pltpu.VMEM((1, NCELL), jnp.int32),
            pltpu.VMEM((1, PHASES), f32),
            pltpu.VMEM((1, SNAP), f32),
            pltpu.VMEM((NBASIS, SNAP), f32),
            pltpu.VMEM((NCELL, NCELL), bf),
            pltpu.VMEM((SNAP, NCELL), bf),
            pltpu.VMEM((SNAP, NCELL), bf),
            pltpu.VMEM((SNAP, 3 * NCELL), bf),
            pltpu.VMEM((3, PACK, 128), bf),
            pltpu.VMEM((3, PACK, 128), bf),
            pltpu.VMEM((4 * NBASIS, SNAP), f32),
            pltpu.VMEM((3, NBASIS, SNAP), f32),
            pltpu.VMEM((N, W), f32),
            pltpu.VMEM((NBASIS, SNAP), f32),
            pltpu.VMEM((3, NBASIS, SNAP), f32),
            pltpu.SemaphoreType.DMA((4,)),
            pltpu.SemaphoreType.DMA((1 + len(CHUNKS),)),
            pltpu.SemaphoreType.DMA((3,)),
            pltpu.SemaphoreType.DMA((3,)),
            pltpu.SemaphoreType.DMA((3,)),
            pltpu.SemaphoreType.DMA((3,)),
            pltpu.SemaphoreType.DMA((3,)),
            pltpu.SemaphoreType.DMA((3,)),
        ],
        compiler_params=pltpu.CompilerParams(collective_id=0, has_side_effects=True),
        name="basis",
    )(phase_labels, phase_perm.reshape(1, PHASES), local_inverse, sources, shift, probe.T)
    coef, element = pl.pallas_call(
        scale_kernel, out_shape=shapes, in_specs=[VMEM, VMEM], out_specs=(VMEM, VMEM), name="scale",
    )(coef, element)
    return (coef.transpose(0, 2, 1), element)


def solution(mesh):
    size = (mesh.shape["grp"], mesh.shape["sub"])
    in_specs = (
        P(("grp", "sub"), None),
        P(),
        P(("grp", "sub"), None, None),
        P(("grp", "sub"), None, None),
        P(("grp", "sub"), None),
        P(),
    )
    out_specs = (P(("grp", "sub"), None, None), P(("grp", "sub"), None, None))
    return jax.shard_map(functools.partial(local, size), mesh=mesh, in_specs=in_specs, out_specs=out_specs, check_vma=False)
```

```python
import functools
import jax
import jax.numpy as jnp
from jax import lax
from jax.experimental import pallas as pl
from jax.experimental.pallas import tpu as pltpu
from jax.sharding import PartitionSpec as P

HI = lax.Precision.HIGHEST
N = 256
NB = 16
W = 384
NBASIS = 8
bf, f32 = jnp.bfloat16, jnp.float32


def spread(group, row):
    return jnp.broadcast_to(group[row:row + 1], (8, 128))


def leaf(cols, slabs):
    row = lax.broadcasted_iota(jnp.int32, (8, 128), 0)
    cols, slabs = list(cols), list(slabs)
    for p in range(0, NB, 2):
        g, i = p // 8, p % 8
        c0, c1 = cols[p], cols[p + 1]
        a, b = spread(c0[g], i), spread(c1[g], i)
        bt, d = spread(c0[g], i + 1), spread(c1[g], i + 1)
        inv = 1.0 / (a * d - b * bt)
        a, b, bt, d = a * inv, b * inv, bt * inv, d * inv
        e0 = [x * d - y * bt for x, y in zip(c0, c1)]
        e1 = [y * a - x * b for x, y in zip(c0, c1)]
        first, second = row == i, row == i + 1
        e0[g] = jnp.where(first, -d, jnp.where(second, bt, e0[g]))
        e1[g] = jnp.where(first, b, jnp.where(second, -a, e1[g]))
        pair = (row == i) | (row == i + 1)

        def step(t):
            r0, r1 = spread(t[g], i), spread(t[g], i + 1)
            z = list(t)
            z[g] = jnp.where(pair, 0.0, t[g])
            return [x - u * r0 - v * r1 for x, u, v in zip(z, e0, e1)]

        for q in range(p + 2, NB):
            cols[q] = step(cols[q])
        slabs = [step(t) for t in slabs]
    return slabs


def halves(x):
    hi = x.astype(bf)
    return hi, (x - hi.astype(f32)).astype(bf)


def column(tile, off, q):
    return [jnp.broadcast_to(t[:, off + q:off + q + 1], (8, 128)) for t in tile]


def eliminate(m_ref):
    steps = N // NB
    tile = lambda k: (k * NB) // 128
    low8 = lambda rows: lax.broadcasted_iota(jnp.int32, (rows, 128), 1) < NBASIS

    def moved(k, pieces):
        if k == 0:
            return {0: jnp.where(low8(pieces[0].shape[0]), pieces[2], pieces[0]), 1: pieces[1]}
        if k == 8:
            return {1: jnp.where(low8(pieces[1].shape[0]), pieces[0], pieces[1])}
        return pieces

    def read(k, t):
        return [m_ref[k * NB + 8 * g:k * NB + 8 * g + 8, 128 * t:128 * t + 128] for g in range(2)]

    slab = {t: read(0, t) for t in range(3)}
    for k in range(steps):
        t0, off = tile(k), (k * NB) % 128
        cols = [column(slab[t0], off, q) for q in range(NB)]
        live = [0, 1, 2] if k == 0 else [0, 1] if k <= 8 else [1]
        new = dict(zip(live, leaf(cols, [slab[t] for t in live])))
        if k + 1 < steps:
            factor_tile = read(k + 1, t0)
            factors = [column(factor_tile, off, q) for q in range(NB)]
            nxt = {}
            for t in live:
                rows = [spread(new[t][q // 8], q % 8) for q in range(NB)]
                groups = []
                for g, start in enumerate(read(k + 1, t)):
                    parts = []
                    for c in range(0, NB, 4):
                        s = factors[c][g] * rows[c]
                        for q in range(c + 1, c + 4):
                            s = s + factors[q][g] * rows[q]
                        parts.append(s)
                    groups.append(start - ((parts[0] + parts[1]) + (parts[2] + parts[3])))
                nxt[t] = groups
            both = [moved(k, {t: nxt[t][g] for t in live}) for g in range(2)]
            slab = {t: [both[0][t], both[1][t]] for t in both[0]}
        new = {t: jnp.concatenate(new[t], axis=0) for t in live}
        hi, low = halves(jnp.concatenate([new[t] for t in live], axis=1))
        width = 128 * len(live)
        gap = lambda n: [jnp.zeros((n, width), bf)] if n else []
        right = jnp.concatenate(
            [piece for x in (hi, hi, low, low) for piece in gap(off) + [x] + gap(128 - off - NB)], axis=0)
        lo = live[0] * 128

        def update(r0, r1):
            if r1 <= r0:
                return
            lhi, llow = halves(m_ref[r0:r1, 128 * t0:128 * t0 + 128])
            left = jnp.concatenate([lhi, llow, lhi, llow], axis=1)
            got = m_ref[r0:r1, lo:lo + width] - jnp.dot(left, right, preferred_element_type=f32)
            pieces = moved(k, {t: got[:, 128 * i:128 * i + 128] for i, t in enumerate(live)})
            for t in pieces:
                m_ref[r0:r1, 128 * t:128 * t + 128] = pieces[t]

        update((k + 2) * NB, N)
        update(0, k * NB)
        pieces = moved(k, new)
        for t in pieces:
            m_ref[k * NB:(k + 1) * NB, 128 * t:128 * t + 128] = pieces[t]


CELLX, CELLY, CELLZ, SNAP, NBASIS, PHASES, NCELL = 12, 12, 8, 256, 8, 3, 1152
STRIDES = (CELLY * CELLZ, CELLZ, 1)
CHUNKS = ((0, 256), (256, 768), (768, 1152))
PACK = 272
MESH = pl.DeviceIdType.MESH
NT = (((1,), (1,)), ((), ()))
VMEM = pl.BlockSpec(memory_space=pltpu.VMEM)


def ahead(field, stride):
    return pltpu.roll(field, NCELL - stride, axis=1)


def cell_weights():
    cell = lax.broadcasted_iota(jnp.int32, (1, NCELL), 1)
    run = lax.shift_right_logical(cell, 3)
    coord_x = lax.shift_right_logical(run * 683, 13)
    coord_y = run - coord_x * CELLY
    coord_z = lax.bitwise_and(cell, CELLZ - 1)
    fx = (coord_x.astype(f32) + 0.5) * (1.0 / CELLX)
    fy = (coord_y.astype(f32) + 0.5) * (1.0 / CELLY)
    partition = [(1.0 - fx) * (1.0 - fy), fx * (1.0 - fy), (1.0 - fx) * fy, fx * fy]
    inside = [coord_x < CELLX - 1, coord_y < CELLY - 1, coord_z < CELLZ - 1]
    return partition, inside


def permeability(labels_ref, perm_ref, inside):
    labels, perm = labels_ref[...], perm_ref[...]
    kappa = jnp.where(labels == 0, perm[:, 0:1], jnp.where(labels == 1, perm[:, 1:2], perm[:, 2:3]))
    face = []
    for stride, keep in zip(STRIDES, inside):
        other = ahead(kappa, stride)
        face.append(jnp.where(keep, 2.0 * kappa * other / (kappa + other), 0.0))
    return kappa, face


def split3(x):
    hi = x.astype(bf)
    rest = x - hi.astype(f32)
    mid = rest.astype(bf)
    low = (rest - mid.astype(f32)).astype(bf)
    return jnp.concatenate([hi, mid, low], axis=0)


def neighbours(axes_size, step):
    grps, subs = axes_size
    g, s = lax.axis_index("grp"), lax.axis_index("sub")
    g1 = lax.rem(g + grps + step, grps)
    s1 = lax.rem(s + subs + step, subs)
    return [(g, s1), (g1, s), (g1, s1)]


def basis_kernel(size, labels_hbm, perm_hbm, inverse_ref, sources_ref, shift_hbm, probe_hbm,
                 coef_ref, element_ref, labels_ref, perm_ref, shift_ref, probe_ref, inv_ref, src_ref, snap_ref,
                 grad_ref, out_ref, in_ref, side_out_ref, side_in_ref, sum_ref, m_ref, coef_out_ref, coef_in_ref,
                 small_sem, load_sem, send_sem, recv_sem, side_send_sem, side_recv_sem, coef_send_sem, coef_recv_sem):
    onward, back = neighbours(size, 1), neighbours(size, -1)
    loads = [pltpu.make_async_copy(sources_ref.at[0], src_ref, load_sem.at[0])]
    for i, (start, stop) in enumerate(CHUNKS):
        part = pl.ds(start, stop - start)
        loads.append(pltpu.make_async_copy(inverse_ref.at[0, :, part], inv_ref.at[:, part], load_sem.at[i + 1]))
    small = [pltpu.make_async_copy(source, target, small_sem.at[i]) for i, (source, target) in enumerate(
        ((labels_hbm, labels_ref), (perm_hbm, perm_ref), (shift_hbm, shift_ref), (probe_hbm, probe_ref)))]
    for load in loads[:2] + small + loads[2:]:
        load.start()
    barrier = pltpu.get_barrier_semaphore()
    for device in back:
        pl.semaphore_signal(barrier, inc=1, device_id=device, device_id_type=MESH)

    volume = 1.0 / NCELL
    partition, inside = cell_weights()
    for load in small:
        load.wait()
    kappa, face = permeability(labels_ref, perm_ref, inside)
    half = [f * (0.5 * volume) for f in face]
    weights = [jnp.concatenate([h * (p + ahead(p, s)) for h, s in zip(half, STRIDES)], axis=1).astype(bf)
               for p in partition]
    probe_rows = split3(probe_ref[...])

    loads[0].wait()
    for i, (start, stop) in enumerate(CHUNKS):
        loads[i + 1].wait()
        snap_ref[:, start:stop] = jnp.dot(
            src_ref[...], inv_ref[:, start:stop], preferred_element_type=f32).astype(bf)
    for r in range(0, SNAP, 64):
        field = snap_ref[r:r + 64, :]
        for d, stride in enumerate(STRIDES):
            grad_ref[r:r + 64, d * NCELL:(d + 1) * NCELL] = ahead(field, stride) - field

    row = lax.broadcasted_iota(jnp.int32, (128, 128), 0)
    col = lax.broadcasted_iota(jnp.int32, (128, 128), 1)

    def gram(corner):
        g = lax.dot_general(grad_ref[...] * weights[corner], grad_ref[...], NT, preferred_element_type=f32)
        first, below, second = g[:128, :128], g[128:, :128], g[128:, 128:]
        diagonal = jnp.sum(jnp.where(row == col, second, 0.0), axis=0, keepdims=True)
        return [jnp.where(row >= col, first, second), below, diagonal]

    def remote(sources, targets, slot, send, recv, device):
        return pltpu.make_async_remote_copy(
            src_ref=sources, dst_ref=targets.at[slot], send_sem=send.at[slot], recv_sem=recv.at[slot],
            device_id=device, device_id_type=MESH)

    def pack(slot, square, below, diagonal):
        out_ref[slot, 0:128, :] = square.astype(bf)
        out_ref[slot, 128:256, :] = below.astype(bf)
        out_ref[slot, 256:272, :] = jnp.broadcast_to(diagonal, (16, 128)).astype(bf)

    def plus(slot, square, below, diagonal):
        return (square + in_ref[slot, 0:128, :].astype(f32), below + in_ref[slot, 128:256, :].astype(f32),
                diagonal + in_ref[slot, 256:272, :].astype(f32)[0:1])

    grps, subs = size
    g, s = lax.axis_index("grp"), lax.axis_index("sub")
    parity = lax.rem(s, 2)
    far = (lax.rem(g + parity, grps), lax.rem(s + 1, subs))
    across = [remote(out_ref.at[slot], in_ref, slot, send_sem, recv_sem, device)
              for slot, device in enumerate((onward[0], onward[1], far))]
    both = gram(3), gram(2)
    pack(2, *both[0])
    pl.semaphore_wait(barrier, 3)
    across[2].start()

    @pl.when(parity == 0)
    def _():
        pack(1, *both[1])
        across[1].start()

    probed = jnp.dot(probe_rows, snap_ref[...], preferred_element_type=f32)
    probed = probed[0:8] + probed[8:16] + probed[16:24]
    heavy = kappa * volume
    loaded = jnp.concatenate([probed * (heavy * p) for p in partition], axis=0)
    side = lax.dot_general(split3(loaded), snap_ref[...], NT, preferred_element_type=f32)
    side = side[0:32] + side[32:64] + side[64:96]
    side_out_ref[...] = side
    sides = []
    for slot in (2, 1, 0):
        corner = slot + 1
        sides.append(remote(side_out_ref.at[pl.ds(8 * corner, 8)], side_in_ref, slot, side_send_sem, side_recv_sem,
                            onward[slot]))
        sides[-1].start()

    @pl.when(parity == 1)
    def _():
        across[2].wait_recv()
        pack(1, *plus(2, *both[1]))
        across[1].start()

    beside, own = gram(1), gram(0)
    pack(0, *beside)
    across[2].wait_send()
    across[1].wait_send()
    across[0].start()
    own_side = side[0:8]
    for copy in sides:
        copy.wait_recv()
    own_side = own_side + (side_in_ref[0] + side_in_ref[1] + side_in_ref[2])
    for slot in (0, 1):
        across[slot].wait_recv()
        own = plus(slot, *own)
    sum_ref[0:128, :] = own[0]
    sum_ref[128:256, :] = own[1]
    sum_ref[256:264, :] = jnp.broadcast_to(own[2], (8, 128))

    @pl.when(parity == 0)
    def _():
        across[2].wait_recv()
        sum_ref[...] = sum_ref[...] + in_ref[2, 0:264, :].astype(f32)

    square, below, diagonal = sum_ref[0:128, :], sum_ref[128:256, :], sum_ref[256:257, :]
    turned = square.T
    shift = shift_ref[...]
    m_ref[:128, :128] = jnp.where(row >= col, square, turned) + jnp.where(row == col, shift[:, :128], 0.0)
    m_ref[128:, :128] = below
    m_ref[:128, 128:256] = below.T
    m_ref[128:, 128:256] = jnp.where(
        row == col, diagonal + shift[:, 128:], jnp.where(row < col, square, turned))
    m_ref[:, N:] = jnp.concatenate([own_side, jnp.zeros((120, SNAP), f32)], axis=0).T
    eliminate(m_ref)

    solved = m_ref[:, 128:256].T[0:8]
    coef_ref[0] = solved
    own = solved.astype(bf).astype(f32)
    coef_out_ref[...] = own
    sends = []
    for slot in (2, 1, 0):
        sends.append(pltpu.make_async_remote_copy(
            src_ref=coef_out_ref, dst_ref=coef_in_ref.at[slot], send_sem=coef_send_sem.at[slot],
            recv_sem=coef_recv_sem.at[slot], device_id=back[slot], device_id_type=MESH))
        sends[-1].start()
    for send in sends:
        send.wait_recv()
    corners = jnp.concatenate([own, coef_in_ref[0], coef_in_ref[1], coef_in_ref[2]], axis=0).astype(bf)
    field = jnp.dot(corners, snap_ref[...], preferred_element_type=f32)
    field = jnp.concatenate([field[8 * c:8 * c + 8] * partition[c] for c in range(4)], axis=0)
    slopes = [ahead(field, stride) - field for stride in STRIDES]
    left = jnp.concatenate(halves(jnp.concatenate([s * f for s, f in zip(slopes, face)], axis=1)), axis=0)
    right = jnp.concatenate(halves(jnp.concatenate(slopes, axis=1)), axis=0)
    product = (lax.dot_general(left[:, :1792], right[:, :1792], NT, preferred_element_type=f32)
               + lax.dot_general(left[:, 1792:], right[:, 1792:], NT, preferred_element_type=f32))
    product = product[0:32] + product[32:64]
    element_ref[0] = product[:, 0:32] + product[:, 32:64]
    for copy in across[:1] + sides + sends:
        copy.wait_send()


def scale_kernel(coef_ref, element_ref, coef_out_ref, element_out_ref):
    coef_out_ref[...] = coef_ref[...]
    element_out_ref[...] = element_ref[...] * (1.0 / (NCELL * SNAP))


def local(size, phase_labels, phase_perm, local_inverse, sources, shift, probe):
    shapes = (jax.ShapeDtypeStruct((1, NBASIS, SNAP), f32), jax.ShapeDtypeStruct((1, 32, 32), f32))
    coef, element = pl.pallas_call(
        functools.partial(basis_kernel, size),
        out_shape=shapes,
        in_specs=[pl.BlockSpec(memory_space=pl.ANY)] * 6,
        out_specs=(VMEM, VMEM),
        scratch_shapes=[
            pltpu.VMEM((1, NCELL), jnp.int32),
            pltpu.VMEM((1, PHASES), f32),
            pltpu.VMEM((1, SNAP), f32),
            pltpu.VMEM((NBASIS, SNAP), f32),
            pltpu.VMEM((NCELL, NCELL), bf),
            pltpu.VMEM((SNAP, NCELL), bf),
            pltpu.VMEM((SNAP, NCELL), bf),
            pltpu.VMEM((SNAP, 3 * NCELL), bf),
            pltpu.VMEM((3, PACK, 128), bf),
            pltpu.VMEM((3, PACK, 128), bf),
            pltpu.VMEM((4 * NBASIS, SNAP), f32),
            pltpu.VMEM((3, NBASIS, SNAP), f32),
            pltpu.VMEM((264, 128), f32),
            pltpu.VMEM((N, W), f32),
            pltpu.VMEM((NBASIS, SNAP), f32),
            pltpu.VMEM((3, NBASIS, SNAP), f32),
            pltpu.SemaphoreType.DMA((4,)),
            pltpu.SemaphoreType.DMA((1 + len(CHUNKS),)),
            pltpu.SemaphoreType.DMA((3,)),
            pltpu.SemaphoreType.DMA((3,)),
            pltpu.SemaphoreType.DMA((3,)),
            pltpu.SemaphoreType.DMA((3,)),
            pltpu.SemaphoreType.DMA((3,)),
            pltpu.SemaphoreType.DMA((3,)),
        ],
        compiler_params=pltpu.CompilerParams(collective_id=0, has_side_effects=True),
        name="basis",
    )(phase_labels, phase_perm.reshape(1, PHASES), local_inverse, sources, shift, probe.T)
    coef, element = pl.pallas_call(
        scale_kernel, out_shape=shapes, in_specs=[VMEM, VMEM], out_specs=(VMEM, VMEM), name="scale",
    )(coef, element)
    return (coef.transpose(0, 2, 1), element)


def solution(mesh):
    size = (mesh.shape["grp"], mesh.shape["sub"])
    in_specs = (
        P(("grp", "sub"), None),
        P(),
        P(("grp", "sub"), None, None),
        P(("grp", "sub"), None, None),
        P(("grp", "sub"), None),
        P(),
    )
    out_specs = (P(("grp", "sub"), None, None), P(("grp", "sub"), None, None))
    return jax.shard_map(functools.partial(local, size), mesh=mesh, in_specs=in_specs, out_specs=out_specs, check_vma=False)
```

```python
import functools
import jax
import jax.numpy as jnp
from jax import lax
from jax.experimental import pallas as pl
from jax.experimental.pallas import tpu as pltpu
from jax.sharding import PartitionSpec as P

HI = lax.Precision.HIGHEST
N = 256
NB = 16
W = 384
NBASIS = 8
bf, f32 = jnp.bfloat16, jnp.float32


def spread(group, row):
    return jnp.broadcast_to(group[row:row + 1], (8, 128))


def leaf(cols, slabs):
    row = lax.broadcasted_iota(jnp.int32, (8, 128), 0)
    cols, slabs = list(cols), list(slabs)
    for p in range(0, NB, 2):
        g, i = p // 8, p % 8
        c0, c1 = cols[p], cols[p + 1]
        a, b = spread(c0[g], i), spread(c1[g], i)
        bt, d = spread(c0[g], i + 1), spread(c1[g], i + 1)
        inv = 1.0 / (a * d - b * bt)
        a, b, bt, d = a * inv, b * inv, bt * inv, d * inv
        e0 = [x * d - y * bt for x, y in zip(c0, c1)]
        e1 = [y * a - x * b for x, y in zip(c0, c1)]
        first, second = row == i, row == i + 1
        e0[g] = jnp.where(first, -d, jnp.where(second, bt, e0[g]))
        e1[g] = jnp.where(first, b, jnp.where(second, -a, e1[g]))
        pair = (row == i) | (row == i + 1)

        def step(t):
            r0, r1 = spread(t[g], i), spread(t[g], i + 1)
            z = list(t)
            z[g] = jnp.where(pair, 0.0, t[g])
            return [x - u * r0 - v * r1 for x, u, v in zip(z, e0, e1)]

        for q in range(p + 2, NB):
            cols[q] = step(cols[q])
        slabs = [step(t) for t in slabs]
    return slabs


def halves(x):
    hi = x.astype(bf)
    return hi, (x - hi.astype(f32)).astype(bf)


def column(tile, off, q):
    return [jnp.broadcast_to(t[:, off + q:off + q + 1], (8, 128)) for t in tile]


def eliminate(m_ref):
    steps = N // NB
    tile = lambda k: (k * NB) // 128
    low8 = lambda rows: lax.broadcasted_iota(jnp.int32, (rows, 128), 1) < NBASIS

    def moved(k, pieces):
        if k == 0:
            return {0: jnp.where(low8(pieces[0].shape[0]), pieces[2], pieces[0]), 1: pieces[1]}
        if k == 8:
            return {1: jnp.where(low8(pieces[1].shape[0]), pieces[0], pieces[1])}
        return pieces

    def read(k, t):
        return [m_ref[k * NB + 8 * g:k * NB + 8 * g + 8, 128 * t:128 * t + 128] for g in range(2)]

    slab = {t: read(0, t) for t in range(3)}
    for k in range(steps):
        t0, off = tile(k), (k * NB) % 128
        cols = [column(slab[t0], off, q) for q in range(NB)]
        live = [0, 1, 2] if k == 0 else [0, 1] if k <= 8 else [1]
        new = dict(zip(live, leaf(cols, [slab[t] for t in live])))
        if k + 1 < steps:
            factor_tile = read(k + 1, t0)
            factors = [column(factor_tile, off, q) for q in range(NB)]
            nxt = {}
            for t in live:
                rows = [spread(new[t][q // 8], q % 8) for q in range(NB)]
                groups = []
                for g, start in enumerate(read(k + 1, t)):
                    parts = []
                    for c in range(0, NB, 4):
                        s = factors[c][g] * rows[c]
                        for q in range(c + 1, c + 4):
                            s = s + factors[q][g] * rows[q]
                        parts.append(s)
                    groups.append(start - ((parts[0] + parts[1]) + (parts[2] + parts[3])))
                nxt[t] = groups
            both = [moved(k, {t: nxt[t][g] for t in live}) for g in range(2)]
            slab = {t: [both[0][t], both[1][t]] for t in both[0]}
        new = {t: jnp.concatenate(new[t], axis=0) for t in live}
        hi, low = halves(jnp.concatenate([new[t] for t in live], axis=1))
        width = 128 * len(live)
        gap = lambda n: [jnp.zeros((n, width), bf)] if n else []
        right = jnp.concatenate(
            [piece for x in (hi, hi, low, low) for piece in gap(off) + [x] + gap(128 - off - NB)], axis=0)
        lo = live[0] * 128

        def update(r0, r1):
            if r1 <= r0:
                return
            lhi, llow = halves(m_ref[r0:r1, 128 * t0:128 * t0 + 128])
            left = jnp.concatenate([lhi, llow, lhi, llow], axis=1)
            got = m_ref[r0:r1, lo:lo + width] - jnp.dot(left, right, preferred_element_type=f32)
            pieces = moved(k, {t: got[:, 128 * i:128 * i + 128] for i, t in enumerate(live)})
            for t in pieces:
                m_ref[r0:r1, 128 * t:128 * t + 128] = pieces[t]

        update((k + 2) * NB, N)
        update(0, k * NB)
        pieces = moved(k, new)
        for t in pieces:
            m_ref[k * NB:(k + 1) * NB, 128 * t:128 * t + 128] = pieces[t]


CELLX, CELLY, CELLZ, SNAP, NBASIS, PHASES, NCELL = 12, 12, 8, 256, 8, 3, 1152
STRIDES = (CELLY * CELLZ, CELLZ, 1)
CHUNKS = ((0, 256), (256, 768), (768, 1152))
PACK = 272
MESH = pl.DeviceIdType.MESH
NT = (((1,), (1,)), ((), ()))
VMEM = pl.BlockSpec(memory_space=pltpu.VMEM)


def ahead(field, stride):
    return pltpu.roll(field, NCELL - stride, axis=1)


def cell_weights():
    cell = lax.broadcasted_iota(jnp.int32, (1, NCELL), 1)
    run = lax.shift_right_logical(cell, 3)
    coord_x = lax.shift_right_logical(run * 683, 13)
    coord_y = run - coord_x * CELLY
    coord_z = lax.bitwise_and(cell, CELLZ - 1)
    fx = (coord_x.astype(f32) + 0.5) * (1.0 / CELLX)
    fy = (coord_y.astype(f32) + 0.5) * (1.0 / CELLY)
    partition = [(1.0 - fx) * (1.0 - fy), fx * (1.0 - fy), (1.0 - fx) * fy, fx * fy]
    inside = [coord_x < CELLX - 1, coord_y < CELLY - 1, coord_z < CELLZ - 1]
    return partition, inside


def permeability(labels_ref, perm_ref, inside):
    labels, perm = labels_ref[...], perm_ref[...]
    kappa = jnp.where(labels == 0, perm[:, 0:1], jnp.where(labels == 1, perm[:, 1:2], perm[:, 2:3]))
    face = []
    for stride, keep in zip(STRIDES, inside):
        other = ahead(kappa, stride)
        face.append(jnp.where(keep, 2.0 * kappa * other / (kappa + other), 0.0))
    return kappa, face


def split3(x):
    hi = x.astype(bf)
    rest = x - hi.astype(f32)
    mid = rest.astype(bf)
    low = (rest - mid.astype(f32)).astype(bf)
    return jnp.concatenate([hi, mid, low], axis=0)


def neighbours(axes_size, step):
    grps, subs = axes_size
    g, s = lax.axis_index("grp"), lax.axis_index("sub")
    g1 = lax.rem(g + grps + step, grps)
    s1 = lax.rem(s + subs + step, subs)
    return [(g, s1), (g1, s), (g1, s1)]


def basis_kernel(size, labels_hbm, perm_hbm, inverse_ref, sources_ref, shift_hbm, probe_hbm,
                 coef_ref, element_ref, labels_ref, perm_ref, shift_ref, probe_ref, inv_ref, src_ref, snap_ref,
                 grad_ref, out_ref, in_ref, side_out_ref, side_in_ref, sum_ref, m_ref, coef_out_ref, coef_in_ref,
                 small_sem, load_sem, send_sem, recv_sem, side_send_sem, side_recv_sem, coef_send_sem, coef_recv_sem):
    onward, back = neighbours(size, 1), neighbours(size, -1)
    loads = [pltpu.make_async_copy(sources_ref.at[0], src_ref, load_sem.at[0])]
    for i, (start, stop) in enumerate(CHUNKS):
        part = pl.ds(start, stop - start)
        loads.append(pltpu.make_async_copy(inverse_ref.at[0, :, part], inv_ref.at[:, part], load_sem.at[i + 1]))
    small = [pltpu.make_async_copy(source, target, small_sem.at[i]) for i, (source, target) in enumerate(
        ((labels_hbm, labels_ref), (perm_hbm, perm_ref), (shift_hbm, shift_ref), (probe_hbm, probe_ref)))]
    for load in loads[:2] + small + loads[2:]:
        load.start()
    barrier = pltpu.get_barrier_semaphore()
    for device in back:
        pl.semaphore_signal(barrier, inc=1, device_id=device, device_id_type=MESH)

    volume = 1.0 / NCELL

    def snapshots(start, stop):
        snap_ref[:, start:stop] = jnp.dot(
            src_ref[...], inv_ref[:, start:stop], preferred_element_type=f32).astype(bf)

    for load in loads[:2] + small:
        load.wait()
    snapshots(*CHUNKS[0])
    partition, inside = cell_weights()
    kappa, face = permeability(labels_ref, perm_ref, inside)
    half = [f * (0.5 * volume) for f in face]
    weights = [jnp.concatenate([h * (p + ahead(p, s)) for h, s in zip(half, STRIDES)], axis=1).astype(bf)
               for p in partition]
    probe_rows = split3(probe_ref[...])
    for load, chunk in zip(loads[2:], CHUNKS[1:]):
        load.wait()
        snapshots(*chunk)
    for d, stride in enumerate(STRIDES):
        for r in range(0, SNAP, 64):
            field = snap_ref[r:r + 64, :]
            grad_ref[r:r + 64, d * NCELL:(d + 1) * NCELL] = ahead(field, stride) - field

    row = lax.broadcasted_iota(jnp.int32, (128, 128), 0)
    col = lax.broadcasted_iota(jnp.int32, (128, 128), 1)

    def gram(corner):
        g = lax.dot_general(grad_ref[...] * weights[corner], grad_ref[...], NT, preferred_element_type=f32)
        first, below, second = g[:128, :128], g[128:, :128], g[128:, 128:]
        diagonal = jnp.sum(jnp.where(row == col, second, 0.0), axis=0, keepdims=True)
        return [jnp.where(row >= col, first, second), below, diagonal]

    def remote(sources, targets, slot, send, recv, device):
        return pltpu.make_async_remote_copy(
            src_ref=sources, dst_ref=targets.at[slot], send_sem=send.at[slot], recv_sem=recv.at[slot],
            device_id=device, device_id_type=MESH)

    def pack(slot, square, below, diagonal):
        out_ref[slot, 0:128, :] = square.astype(bf)
        out_ref[slot, 128:256, :] = below.astype(bf)
        out_ref[slot, 256:272, :] = jnp.broadcast_to(diagonal, (16, 128)).astype(bf)

    def plus(slot, square, below, diagonal):
        return (square + in_ref[slot, 0:128, :].astype(f32), below + in_ref[slot, 128:256, :].astype(f32),
                diagonal + in_ref[slot, 256:272, :].astype(f32)[0:1])

    grps, subs = size
    g, s = lax.axis_index("grp"), lax.axis_index("sub")
    parity = lax.rem(s, 2)
    far = (lax.rem(g + parity, grps), lax.rem(s + 1, subs))
    across = [remote(out_ref.at[slot], in_ref, slot, send_sem, recv_sem, device)
              for slot, device in enumerate((onward[0], onward[1], far))]
    both = gram(3), gram(2)
    pack(2, *both[0])
    pl.semaphore_wait(barrier, 3)
    across[2].start()

    @pl.when(parity == 0)
    def _():
        pack(1, *both[1])
        across[1].start()

    probed = jnp.dot(probe_rows, snap_ref[...], preferred_element_type=f32)
    probed = probed[0:8] + probed[8:16] + probed[16:24]
    heavy = kappa * volume
    loaded = jnp.concatenate([probed * (heavy * p) for p in partition], axis=0)
    side = lax.dot_general(split3(loaded), snap_ref[...], NT, preferred_element_type=f32)
    side = side[0:32] + side[32:64] + side[64:96]
    side_out_ref[...] = side
    sides = []
    for slot in (2, 1, 0):
        corner = slot + 1
        sides.append(remote(side_out_ref.at[pl.ds(8 * corner, 8)], side_in_ref, slot, side_send_sem, side_recv_sem,
                            onward[slot]))
        sides[-1].start()

    @pl.when(parity == 1)
    def _():
        across[2].wait_recv()
        pack(1, *plus(2, *both[1]))
        across[1].start()

    beside, own = gram(1), gram(0)
    pack(0, *beside)
    across[2].wait_send()
    across[1].wait_send()
    across[0].start()
    own_side = side[0:8]
    for copy in sides:
        copy.wait_recv()
    own_side = own_side + (side_in_ref[0] + side_in_ref[1] + side_in_ref[2])
    for slot in (0, 1):
        across[slot].wait_recv()
        own = plus(slot, *own)
    sum_ref[0:128, :] = own[0]
    sum_ref[128:256, :] = own[1]
    sum_ref[256:264, :] = jnp.broadcast_to(own[2], (8, 128))

    @pl.when(parity == 0)
    def _():
        across[2].wait_recv()
        sum_ref[...] = sum_ref[...] + in_ref[2, 0:264, :].astype(f32)

    square, below, diagonal = sum_ref[0:128, :], sum_ref[128:256, :], sum_ref[256:257, :]
    turned = square.T
    shift = shift_ref[...]
    m_ref[:128, :128] = jnp.where(row >= col, square, turned) + jnp.where(row == col, shift[:, :128], 0.0)
    m_ref[128:, :128] = below
    m_ref[:128, 128:256] = below.T
    m_ref[128:, 128:256] = jnp.where(
        row == col, diagonal + shift[:, 128:], jnp.where(row < col, square, turned))
    m_ref[:, N:] = jnp.concatenate([own_side, jnp.zeros((120, SNAP), f32)], axis=0).T
    eliminate(m_ref)

    solved = m_ref[:, 128:256].T[0:8]
    coef_ref[0] = solved
    own = solved.astype(bf).astype(f32)
    coef_out_ref[...] = own
    sends = []
    for slot in (2, 1, 0):
        sends.append(pltpu.make_async_remote_copy(
            src_ref=coef_out_ref, dst_ref=coef_in_ref.at[slot], send_sem=coef_send_sem.at[slot],
            recv_sem=coef_recv_sem.at[slot], device_id=back[slot], device_id_type=MESH))
        sends[-1].start()
    for send in sends:
        send.wait_recv()
    corners = jnp.concatenate([own, coef_in_ref[0], coef_in_ref[1], coef_in_ref[2]], axis=0).astype(bf)
    field = jnp.dot(corners, snap_ref[...], preferred_element_type=f32)
    field = jnp.concatenate([field[8 * c:8 * c + 8] * partition[c] for c in range(4)], axis=0)
    slopes = [ahead(field, stride) - field for stride in STRIDES]
    left = jnp.concatenate(halves(jnp.concatenate([s * f for s, f in zip(slopes, face)], axis=1)), axis=0)
    right = jnp.concatenate(halves(jnp.concatenate(slopes, axis=1)), axis=0)
    product = (lax.dot_general(left[:, :1792], right[:, :1792], NT, preferred_element_type=f32)
               + lax.dot_general(left[:, 1792:], right[:, 1792:], NT, preferred_element_type=f32))
    product = product[0:32] + product[32:64]
    element_ref[0] = (product[:, 0:32] + product[:, 32:64]) * (1.0 / (NCELL * SNAP))
    for copy in across[:1] + sides + sends:
        copy.wait_send()


def local(size, phase_labels, phase_perm, local_inverse, sources, shift, probe):
    shapes = (jax.ShapeDtypeStruct((1, NBASIS, SNAP), f32), jax.ShapeDtypeStruct((1, 32, 32), f32))
    coef, element = pl.pallas_call(
        functools.partial(basis_kernel, size),
        out_shape=tuple(pltpu.VMEM(shape.shape, shape.dtype) for shape in shapes),
        in_specs=[pl.BlockSpec(memory_space=pl.ANY)] * 6,
        out_specs=(VMEM, VMEM),
        scratch_shapes=[
            pltpu.VMEM((1, NCELL), jnp.int32),
            pltpu.VMEM((1, PHASES), f32),
            pltpu.VMEM((1, SNAP), f32),
            pltpu.VMEM((NBASIS, SNAP), f32),
            pltpu.VMEM((NCELL, NCELL), bf),
            pltpu.VMEM((SNAP, NCELL), bf),
            pltpu.VMEM((SNAP, NCELL), bf),
            pltpu.VMEM((SNAP, 3 * NCELL), bf),
            pltpu.VMEM((3, PACK, 128), bf),
            pltpu.VMEM((3, PACK, 128), bf),
            pltpu.VMEM((4 * NBASIS, SNAP), f32),
            pltpu.VMEM((3, NBASIS, SNAP), f32),
            pltpu.VMEM((264, 128), f32),
            pltpu.VMEM((N, W), f32),
            pltpu.VMEM((NBASIS, SNAP), f32),
            pltpu.VMEM((3, NBASIS, SNAP), f32),
            pltpu.SemaphoreType.DMA((4,)),
            pltpu.SemaphoreType.DMA((1 + len(CHUNKS),)),
            pltpu.SemaphoreType.DMA((3,)),
            pltpu.SemaphoreType.DMA((3,)),
            pltpu.SemaphoreType.DMA((3,)),
            pltpu.SemaphoreType.DMA((3,)),
            pltpu.SemaphoreType.DMA((3,)),
            pltpu.SemaphoreType.DMA((3,)),
        ],
        compiler_params=pltpu.CompilerParams(collective_id=0, has_side_effects=True),
        name="basis",
    )(phase_labels, phase_perm.reshape(1, PHASES), local_inverse, sources, shift, probe.T)
    return (coef.transpose(0, 2, 1), element)


def solution(mesh):
    size = (mesh.shape["grp"], mesh.shape["sub"])
    in_specs = (
        P(("grp", "sub"), None),
        P(),
        P(("grp", "sub"), None, None),
        P(("grp", "sub"), None, None),
        P(("grp", "sub"), None),
        P(),
    )
    out_specs = (P(("grp", "sub"), None, None), P(("grp", "sub"), None, None))
    return jax.shard_map(functools.partial(local, size), mesh=mesh, in_specs=in_specs, out_specs=out_specs, check_vma=False)
```

```python
import functools
import jax
import jax.numpy as jnp
from jax import lax
from jax.experimental import pallas as pl
from jax.experimental.pallas import tpu as pltpu
from jax.sharding import PartitionSpec as P

HI = lax.Precision.HIGHEST
N = 256
NB = 16
W = 384
NBASIS = 8
bf, f32 = jnp.bfloat16, jnp.float32


def spread(group, row):
    return jnp.broadcast_to(group[row:row + 1], (8, 128))


def leaf(cols, slabs):
    row = lax.broadcasted_iota(jnp.int32, (8, 128), 0)
    cols, slabs = list(cols), list(slabs)
    for p in range(0, NB, 2):
        g, i = p // 8, p % 8
        c0, c1 = cols[p], cols[p + 1]
        a, b = spread(c0[g], i), spread(c1[g], i)
        bt, d = spread(c0[g], i + 1), spread(c1[g], i + 1)
        inv = 1.0 / (a * d - b * bt)
        a, b, bt, d = a * inv, b * inv, bt * inv, d * inv
        e0 = [x * d - y * bt for x, y in zip(c0, c1)]
        e1 = [y * a - x * b for x, y in zip(c0, c1)]
        first, second = row == i, row == i + 1
        e0[g] = jnp.where(first, -d, jnp.where(second, bt, e0[g]))
        e1[g] = jnp.where(first, b, jnp.where(second, -a, e1[g]))
        pair = (row == i) | (row == i + 1)

        def step(t):
            r0, r1 = spread(t[g], i), spread(t[g], i + 1)
            z = list(t)
            z[g] = jnp.where(pair, 0.0, t[g])
            return [x - u * r0 - v * r1 for x, u, v in zip(z, e0, e1)]

        for q in range(p + 2, NB):
            cols[q] = step(cols[q])
        slabs = [step(t) for t in slabs]
    return slabs


def halves(x):
    hi = x.astype(bf)
    return hi, (x - hi.astype(f32)).astype(bf)


def column(tile, off, q):
    return [jnp.broadcast_to(t[:, off + q:off + q + 1], (8, 128)) for t in tile]


def eliminate(m_ref):
    steps = N // NB
    tile = lambda k: (k * NB) // 128
    low8 = lambda rows: lax.broadcasted_iota(jnp.int32, (rows, 128), 1) < NBASIS

    def moved(k, pieces):
        if k == 0:
            return {0: jnp.where(low8(pieces[0].shape[0]), pieces[2], pieces[0]), 1: pieces[1]}
        if k == 8:
            return {1: jnp.where(low8(pieces[1].shape[0]), pieces[0], pieces[1])}
        return pieces

    def read(k, t):
        return [m_ref[k * NB + 8 * g:k * NB + 8 * g + 8, 128 * t:128 * t + 128] for g in range(2)]

    slab = {t: read(0, t) for t in range(3)}
    for k in range(steps):
        t0, off = tile(k), (k * NB) % 128
        cols = [column(slab[t0], off, q) for q in range(NB)]
        live = [0, 1, 2] if k == 0 else [0, 1] if k <= 8 else [1]
        new = dict(zip(live, leaf(cols, [slab[t] for t in live])))
        if k + 1 < steps:
            factor_tile = read(k + 1, t0)
            factors = [column(factor_tile, off, q) for q in range(NB)]
            nxt = {}
            for t in live:
                rows = [spread(new[t][q // 8], q % 8) for q in range(NB)]
                groups = []
                for g, start in enumerate(read(k + 1, t)):
                    parts = []
                    for c in range(0, NB, 4):
                        s = factors[c][g] * rows[c]
                        for q in range(c + 1, c + 4):
                            s = s + factors[q][g] * rows[q]
                        parts.append(s)
                    groups.append(start - ((parts[0] + parts[1]) + (parts[2] + parts[3])))
                nxt[t] = groups
            both = [moved(k, {t: nxt[t][g] for t in live}) for g in range(2)]
            slab = {t: [both[0][t], both[1][t]] for t in both[0]}
        new = {t: jnp.concatenate(new[t], axis=0) for t in live}
        hi, low = halves(jnp.concatenate([new[t] for t in live], axis=1))
        width = 128 * len(live)
        gap = lambda n: [jnp.zeros((n, width), bf)] if n else []
        right = jnp.concatenate(
            [piece for x in (hi, hi, low, low) for piece in gap(off) + [x] + gap(128 - off - NB)], axis=0)
        lo = live[0] * 128

        def update(r0, r1):
            if r1 <= r0:
                return
            lhi, llow = halves(m_ref[r0:r1, 128 * t0:128 * t0 + 128])
            left = jnp.concatenate([lhi, llow, lhi, llow], axis=1)
            got = m_ref[r0:r1, lo:lo + width] - jnp.dot(left, right, preferred_element_type=f32)
            pieces = moved(k, {t: got[:, 128 * i:128 * i + 128] for i, t in enumerate(live)})
            for t in pieces:
                m_ref[r0:r1, 128 * t:128 * t + 128] = pieces[t]

        update((k + 2) * NB, N)
        update(0, k * NB)
        pieces = moved(k, new)
        for t in pieces:
            m_ref[k * NB:(k + 1) * NB, 128 * t:128 * t + 128] = pieces[t]


CELLX, CELLY, CELLZ, SNAP, NBASIS, PHASES, NCELL = 12, 12, 8, 256, 8, 3, 1152
STRIDES = (CELLY * CELLZ, CELLZ, 1)
CHUNKS = ((0, 256), (256, 768), (768, 1152))
PACK = 272
MESH = pl.DeviceIdType.MESH
NT = (((1,), (1,)), ((), ()))
VMEM = pl.BlockSpec(memory_space=pltpu.VMEM)


def ahead(field, stride):
    return pltpu.roll(field, NCELL - stride, axis=1)


def cell_weights():
    cell = lax.broadcasted_iota(jnp.int32, (1, NCELL), 1)
    run = lax.shift_right_logical(cell, 3)
    coord_x = lax.shift_right_logical(run * 683, 13)
    coord_y = run - coord_x * CELLY
    coord_z = lax.bitwise_and(cell, CELLZ - 1)
    fx = (coord_x.astype(f32) + 0.5) * (1.0 / CELLX)
    fy = (coord_y.astype(f32) + 0.5) * (1.0 / CELLY)
    partition = [(1.0 - fx) * (1.0 - fy), fx * (1.0 - fy), (1.0 - fx) * fy, fx * fy]
    inside = [coord_x < CELLX - 1, coord_y < CELLY - 1, coord_z < CELLZ - 1]
    return partition, inside


def permeability(labels_ref, perm_ref, inside):
    labels, perm = labels_ref[...], perm_ref[...]
    kappa = jnp.where(labels == 0, perm[:, 0:1], jnp.where(labels == 1, perm[:, 1:2], perm[:, 2:3]))
    face = []
    for stride, keep in zip(STRIDES, inside):
        other = ahead(kappa, stride)
        face.append(jnp.where(keep, 2.0 * kappa * other / (kappa + other), 0.0))
    return kappa, face


def split3(x):
    hi = x.astype(bf)
    rest = x - hi.astype(f32)
    mid = rest.astype(bf)
    low = (rest - mid.astype(f32)).astype(bf)
    return jnp.concatenate([hi, mid, low], axis=0)


def neighbours(axes_size, step):
    grps, subs = axes_size
    g, s = lax.axis_index("grp"), lax.axis_index("sub")
    g1 = lax.rem(g + grps + step, grps)
    s1 = lax.rem(s + subs + step, subs)
    return [(g, s1), (g1, s), (g1, s1)]


def basis_kernel(size, labels_hbm, perm_hbm, inverse_ref, sources_ref, shift_hbm, probe_hbm,
                 coef_ref, element_ref, labels_ref, perm_ref, shift_ref, probe_ref, inv_ref, src_ref, snap_ref,
                 grad_ref, out_ref, in_ref, side_out_ref, side_in_ref, sum_ref, m_ref, coef_out_ref, coef_in_ref,
                 small_sem, load_sem, send_sem, recv_sem, side_send_sem, side_recv_sem, coef_send_sem, coef_recv_sem):
    onward, back = neighbours(size, 1), neighbours(size, -1)
    loads = [pltpu.make_async_copy(sources_ref.at[0], src_ref, load_sem.at[0])]
    for i, (start, stop) in enumerate(CHUNKS):
        part = pl.ds(start, stop - start)
        loads.append(pltpu.make_async_copy(inverse_ref.at[0, :, part], inv_ref.at[:, part], load_sem.at[i + 1]))
    small = [pltpu.make_async_copy(source, target, small_sem.at[i]) for i, (source, target) in enumerate(
        ((labels_hbm, labels_ref), (perm_hbm, perm_ref), (shift_hbm, shift_ref), (probe_hbm, probe_ref)))]
    for load in loads[:2] + small + loads[2:]:
        load.start()
    barrier = pltpu.get_barrier_semaphore()
    for device in back:
        pl.semaphore_signal(barrier, inc=1, device_id=device, device_id_type=MESH)

    volume = 1.0 / NCELL

    def snapshots(start, stop):
        snap_ref[:, start:stop] = jnp.dot(
            src_ref[...], inv_ref[:, start:stop], preferred_element_type=f32).astype(bf)

    for load in loads[:2] + small:
        load.wait()
    snapshots(*CHUNKS[0])
    partition, inside = cell_weights()
    kappa, face = permeability(labels_ref, perm_ref, inside)
    half = [f * (0.5 * volume) for f in face]
    weights = [jnp.concatenate([h * (p + ahead(p, s)) for h, s in zip(half, STRIDES)], axis=1).astype(bf)
               for p in partition]
    probe_rows = split3(probe_ref[...])
    for load, chunk in zip(loads[2:], CHUNKS[1:]):
        load.wait()
        snapshots(*chunk)
    for d, stride in enumerate(STRIDES):
        for r in range(0, SNAP, 64):
            field = snap_ref[r:r + 64, :]
            grad_ref[r:r + 64, d * NCELL:(d + 1) * NCELL] = ahead(field, stride) - field

    row = lax.broadcasted_iota(jnp.int32, (128, 128), 0)
    col = lax.broadcasted_iota(jnp.int32, (128, 128), 1)

    def gram(corner):
        g = lax.dot_general(grad_ref[...] * weights[corner], grad_ref[...], NT, preferred_element_type=f32)
        first, below, second = g[:128, :128], g[128:, :128], g[128:, 128:]
        diagonal = jnp.sum(jnp.where(row == col, second, 0.0), axis=0, keepdims=True)
        return [jnp.where(row >= col, first, second), below, diagonal]

    def remote(sources, targets, slot, send, recv, device):
        return pltpu.make_async_remote_copy(
            src_ref=sources, dst_ref=targets.at[slot], send_sem=send.at[slot], recv_sem=recv.at[slot],
            device_id=device, device_id_type=MESH)

    def pack(slot, square, below, diagonal):
        out_ref[slot, 0:128, :] = square.astype(bf)
        out_ref[slot, 128:256, :] = below.astype(bf)
        out_ref[slot, 256:272, :] = jnp.broadcast_to(diagonal, (16, 128)).astype(bf)

    def plus(slot, square, below, diagonal):
        return (square + in_ref[slot, 0:128, :].astype(f32), below + in_ref[slot, 128:256, :].astype(f32),
                diagonal + in_ref[slot, 256:272, :].astype(f32)[0:1])

    grps, subs = size
    g, s = lax.axis_index("grp"), lax.axis_index("sub")
    parity = lax.rem(s, 2)
    far = (lax.rem(g + parity, grps), lax.rem(s + 1, subs))
    across = [remote(out_ref.at[slot], in_ref, slot, send_sem, recv_sem, device)
              for slot, device in enumerate((onward[0], onward[1], far))]
    both = gram(3), gram(2)
    pack(2, *both[0])
    pl.semaphore_wait(barrier, 3)
    across[2].start()

    @pl.when(parity == 0)
    def _():
        pack(1, *both[1])
        across[1].start()

    probed = jnp.dot(probe_rows, snap_ref[...], preferred_element_type=f32)
    probed = probed[0:8] + probed[8:16] + probed[16:24]
    heavy = kappa * volume
    loaded = jnp.concatenate([probed * (heavy * p) for p in partition], axis=0)
    side = lax.dot_general(split3(loaded), snap_ref[...], NT, preferred_element_type=f32)
    side = side[0:32] + side[32:64] + side[64:96]
    side_out_ref[...] = side
    sides = []
    for slot in (2, 1, 0):
        corner = slot + 1
        sides.append(remote(side_out_ref.at[pl.ds(8 * corner, 8)], side_in_ref, slot, side_send_sem, side_recv_sem,
                            onward[slot]))
        sides[-1].start()

    @pl.when(parity == 1)
    def _():
        across[2].wait_recv()
        pack(1, *plus(2, *both[1]))
        across[1].start()

    beside, own = gram(1), gram(0)
    pack(0, *beside)
    across[2].wait_send()
    across[1].wait_send()
    across[0].start()
    own_side = side[0:8]
    for copy in sides:
        copy.wait_recv()
    own_side = own_side + (side_in_ref[0] + side_in_ref[1] + side_in_ref[2])
    for slot in (0, 1):
        across[slot].wait_recv()
        own = plus(slot, *own)
    sum_ref[0:128, :] = own[0]
    sum_ref[128:256, :] = own[1]
    sum_ref[256:264, :] = jnp.broadcast_to(own[2], (8, 128))

    @pl.when(parity == 0)
    def _():
        across[2].wait_recv()
        sum_ref[...] = sum_ref[...] + in_ref[2, 0:264, :].astype(f32)

    square, below, diagonal = sum_ref[0:128, :], sum_ref[128:256, :], sum_ref[256:257, :]
    turned = square.T
    shift = shift_ref[...]
    m_ref[:128, :128] = jnp.where(row >= col, square, turned) + jnp.where(row == col, shift[:, :128], 0.0)
    m_ref[128:, :128] = below
    m_ref[:128, 128:256] = below.T
    m_ref[128:, 128:256] = jnp.where(
        row == col, diagonal + shift[:, 128:], jnp.where(row < col, square, turned))
    m_ref[:, N:] = jnp.concatenate([own_side, jnp.zeros((120, SNAP), f32)], axis=0).T
    eliminate(m_ref)

    solved = m_ref[:, 128:256].T[0:8]
    coef_ref[0] = solved
    own = solved.astype(bf).astype(f32)
    coef_out_ref[...] = own
    sends = []
    for slot in (2, 1, 0):
        sends.append(pltpu.make_async_remote_copy(
            src_ref=coef_out_ref, dst_ref=coef_in_ref.at[slot], send_sem=coef_send_sem.at[slot],
            recv_sem=coef_recv_sem.at[slot], device_id=back[slot], device_id_type=MESH))
        sends[-1].start()
    for send in sends:
        send.wait_recv()
    corners = jnp.concatenate([own, coef_in_ref[0], coef_in_ref[1], coef_in_ref[2]], axis=0).astype(bf)
    field = jnp.dot(corners, snap_ref[...], preferred_element_type=f32)
    field = jnp.concatenate([field[8 * c:8 * c + 8] * partition[c] for c in range(4)], axis=0)
    slopes = [ahead(field, stride) - field for stride in STRIDES]
    left = jnp.concatenate(halves(jnp.concatenate([s * f for s, f in zip(slopes, face)], axis=1)), axis=0)
    right = jnp.concatenate(halves(jnp.concatenate(slopes, axis=1)), axis=0)
    product = (lax.dot_general(left[:, :1792], right[:, :1792], NT, preferred_element_type=f32)
               + lax.dot_general(left[:, 1792:], right[:, 1792:], NT, preferred_element_type=f32))
    product = product[0:32] + product[32:64]
    element_ref[0] = (product[:, 0:32] + product[:, 32:64]) * (1.0 / (NCELL * SNAP))
    for copy in across[:1] + sides + sends:
        copy.wait_send()


def hand_out_kernel(coef_ref, element_ref, coef_out_ref, element_out_ref, sem):
    copies = [pltpu.make_async_copy(coef_ref, coef_out_ref, sem.at[0]),
              pltpu.make_async_copy(element_ref, element_out_ref, sem.at[1])]
    for copy in copies:
        copy.start()
    for copy in copies:
        copy.wait()


def local(size, phase_labels, phase_perm, local_inverse, sources, shift, probe):
    shapes = (jax.ShapeDtypeStruct((1, NBASIS, SNAP), f32), jax.ShapeDtypeStruct((1, 32, 32), f32))
    coef, element = pl.pallas_call(
        functools.partial(basis_kernel, size),
        out_shape=tuple(pltpu.VMEM(shape.shape, shape.dtype) for shape in shapes),
        in_specs=[pl.BlockSpec(memory_space=pl.ANY)] * 6,
        out_specs=(VMEM, VMEM),
        scratch_shapes=[
            pltpu.VMEM((1, NCELL), jnp.int32),
            pltpu.VMEM((1, PHASES), f32),
            pltpu.VMEM((1, SNAP), f32),
            pltpu.VMEM((NBASIS, SNAP), f32),
            pltpu.VMEM((NCELL, NCELL), bf),
            pltpu.VMEM((SNAP, NCELL), bf),
            pltpu.VMEM((SNAP, NCELL), bf),
            pltpu.VMEM((SNAP, 3 * NCELL), bf),
            pltpu.VMEM((3, PACK, 128), bf),
            pltpu.VMEM((3, PACK, 128), bf),
            pltpu.VMEM((4 * NBASIS, SNAP), f32),
            pltpu.VMEM((3, NBASIS, SNAP), f32),
            pltpu.VMEM((264, 128), f32),
            pltpu.VMEM((N, W), f32),
            pltpu.VMEM((NBASIS, SNAP), f32),
            pltpu.VMEM((3, NBASIS, SNAP), f32),
            pltpu.SemaphoreType.DMA((4,)),
            pltpu.SemaphoreType.DMA((1 + len(CHUNKS),)),
            pltpu.SemaphoreType.DMA((3,)),
            pltpu.SemaphoreType.DMA((3,)),
            pltpu.SemaphoreType.DMA((3,)),
            pltpu.SemaphoreType.DMA((3,)),
            pltpu.SemaphoreType.DMA((3,)),
            pltpu.SemaphoreType.DMA((3,)),
        ],
        compiler_params=pltpu.CompilerParams(collective_id=0, has_side_effects=True),
        name="basis",
    )(phase_labels, phase_perm.reshape(1, PHASES), local_inverse, sources, shift, probe.T)
    coef, element = pl.pallas_call(
        hand_out_kernel,
        out_shape=shapes,
        in_specs=[VMEM, VMEM],
        out_specs=(pl.BlockSpec(memory_space=pl.ANY), pl.BlockSpec(memory_space=pl.ANY)),
        scratch_shapes=[pltpu.SemaphoreType.DMA((2,))],
        name="hand_out",
    )(*(pltpu.with_memory_space_constraint(x, pltpu.VMEM) for x in (coef, element)))
    return (coef.transpose(0, 2, 1), element)


def solution(mesh):
    size = (mesh.shape["grp"], mesh.shape["sub"])
    in_specs = (
        P(("grp", "sub"), None),
        P(),
        P(("grp", "sub"), None, None),
        P(("grp", "sub"), None, None),
        P(("grp", "sub"), None),
        P(),
    )
    out_specs = (P(("grp", "sub"), None, None), P(("grp", "sub"), None, None))
    return jax.shard_map(functools.partial(local, size), mesh=mesh, in_specs=in_specs, out_specs=out_specs, check_vma=False)
```

```python
import functools
import jax
import jax.numpy as jnp
from jax import lax
from jax.experimental import pallas as pl
from jax.experimental.pallas import tpu as pltpu
from jax.sharding import PartitionSpec as P

HI = lax.Precision.HIGHEST
N = 256
NB = 16
W = 384
NBASIS = 8
bf, f32 = jnp.bfloat16, jnp.float32


def spread(group, row):
    return jnp.broadcast_to(group[row:row + 1], (8, 128))


def leaf(cols, slabs):
    row = lax.broadcasted_iota(jnp.int32, (8, 128), 0)
    cols, slabs = list(cols), list(slabs)
    for p in range(0, NB, 2):
        g, i = p // 8, p % 8
        c0, c1 = cols[p], cols[p + 1]
        a, b = spread(c0[g], i), spread(c1[g], i)
        bt, d = spread(c0[g], i + 1), spread(c1[g], i + 1)
        inv = 1.0 / (a * d - b * bt)
        a, b, bt, d = a * inv, b * inv, bt * inv, d * inv
        e0 = [x * d - y * bt for x, y in zip(c0, c1)]
        e1 = [y * a - x * b for x, y in zip(c0, c1)]
        first, second = row == i, row == i + 1
        e0[g] = jnp.where(first, -d, jnp.where(second, bt, e0[g]))
        e1[g] = jnp.where(first, b, jnp.where(second, -a, e1[g]))
        pair = (row == i) | (row == i + 1)

        def step(t):
            r0, r1 = spread(t[g], i), spread(t[g], i + 1)
            z = list(t)
            z[g] = jnp.where(pair, 0.0, t[g])
            return [x - u * r0 - v * r1 for x, u, v in zip(z, e0, e1)]

        for q in range(p + 2, NB):
            cols[q] = step(cols[q])
        slabs = [step(t) for t in slabs]
    return slabs


def halves(x):
    hi = x.astype(bf)
    return hi, (x - hi.astype(f32)).astype(bf)


def column(tile, off, q):
    return [jnp.broadcast_to(t[:, off + q:off + q + 1], (8, 128)) for t in tile]


def eliminate(m_ref):
    steps = N // NB
    tile = lambda k: (k * NB) // 128
    low8 = lambda rows: lax.broadcasted_iota(jnp.int32, (rows, 128), 1) < NBASIS

    def moved(k, pieces):
        if k == 0:
            return {0: jnp.where(low8(pieces[0].shape[0]), pieces[2], pieces[0]), 1: pieces[1]}
        if k == 8:
            return {1: jnp.where(low8(pieces[1].shape[0]), pieces[0], pieces[1])}
        return pieces

    def read(k, t):
        return [m_ref[k * NB + 8 * g:k * NB + 8 * g + 8, 128 * t:128 * t + 128] for g in range(2)]

    slab = {t: read(0, t) for t in range(3)}
    for k in range(steps):
        t0, off = tile(k), (k * NB) % 128
        cols = [column(slab[t0], off, q) for q in range(NB)]
        live = [0, 1, 2] if k == 0 else [0, 1] if k <= 8 else [1]
        new = dict(zip(live, leaf(cols, [slab[t] for t in live])))
        if k + 1 < steps:
            factor_tile = read(k + 1, t0)
            factors = [column(factor_tile, off, q) for q in range(NB)]
            nxt = {}
            for t in live:
                rows = [spread(new[t][q // 8], q % 8) for q in range(NB)]
                groups = []
                for g, start in enumerate(read(k + 1, t)):
                    parts = []
                    for c in range(0, NB, 4):
                        s = factors[c][g] * rows[c]
                        for q in range(c + 1, c + 4):
                            s = s + factors[q][g] * rows[q]
                        parts.append(s)
                    groups.append(start - ((parts[0] + parts[1]) + (parts[2] + parts[3])))
                nxt[t] = groups
            both = [moved(k, {t: nxt[t][g] for t in live}) for g in range(2)]
            slab = {t: [both[0][t], both[1][t]] for t in both[0]}
        new = {t: jnp.concatenate(new[t], axis=0) for t in live}
        hi, low = halves(jnp.concatenate([new[t] for t in live], axis=1))
        width = 128 * len(live)
        gap = lambda n: [jnp.zeros((n, width), bf)] if n else []
        right = jnp.concatenate(
            [piece for x in (hi, hi, low) for piece in gap(off) + [x] + gap(128 - off - NB)], axis=0)
        lo = live[0] * 128

        def update(r0, r1):
            if r1 <= r0:
                return
            lhi, llow = halves(m_ref[r0:r1, 128 * t0:128 * t0 + 128])
            left = jnp.concatenate([lhi, llow, lhi], axis=1)
            got = m_ref[r0:r1, lo:lo + width] - jnp.dot(left, right, preferred_element_type=f32)
            pieces = moved(k, {t: got[:, 128 * i:128 * i + 128] for i, t in enumerate(live)})
            for t in pieces:
                m_ref[r0:r1, 128 * t:128 * t + 128] = pieces[t]

        update((k + 2) * NB, N)
        update(0, k * NB)
        pieces = moved(k, new)
        for t in pieces:
            m_ref[k * NB:(k + 1) * NB, 128 * t:128 * t + 128] = pieces[t]


CELLX, CELLY, CELLZ, SNAP, NBASIS, PHASES, NCELL = 12, 12, 8, 256, 8, 3, 1152
STRIDES = (CELLY * CELLZ, CELLZ, 1)
CHUNKS = ((0, 256), (256, 768), (768, 1152))
PACK = 272
MESH = pl.DeviceIdType.MESH
NT = (((1,), (1,)), ((), ()))
VMEM = pl.BlockSpec(memory_space=pltpu.VMEM)


def ahead(field, stride):
    return pltpu.roll(field, NCELL - stride, axis=1)


def cell_weights():
    cell = lax.broadcasted_iota(jnp.int32, (1, NCELL), 1)
    run = lax.shift_right_logical(cell, 3)
    coord_x = lax.shift_right_logical(run * 683, 13)
    coord_y = run - coord_x * CELLY
    coord_z = lax.bitwise_and(cell, CELLZ - 1)
    fx = (coord_x.astype(f32) + 0.5) * (1.0 / CELLX)
    fy = (coord_y.astype(f32) + 0.5) * (1.0 / CELLY)
    partition = [(1.0 - fx) * (1.0 - fy), fx * (1.0 - fy), (1.0 - fx) * fy, fx * fy]
    inside = [coord_x < CELLX - 1, coord_y < CELLY - 1, coord_z < CELLZ - 1]
    return partition, inside


def permeability(labels_ref, perm_ref, inside):
    labels, perm = labels_ref[...], perm_ref[...]
    kappa = jnp.where(labels == 0, perm[:, 0:1], jnp.where(labels == 1, perm[:, 1:2], perm[:, 2:3]))
    face = []
    for stride, keep in zip(STRIDES, inside):
        other = ahead(kappa, stride)
        face.append(jnp.where(keep, 2.0 * kappa * other / (kappa + other), 0.0))
    return kappa, face


def split3(x):
    hi = x.astype(bf)
    rest = x - hi.astype(f32)
    mid = rest.astype(bf)
    low = (rest - mid.astype(f32)).astype(bf)
    return jnp.concatenate([hi, mid, low], axis=0)


def neighbours(axes_size, step):
    grps, subs = axes_size
    g, s = lax.axis_index("grp"), lax.axis_index("sub")
    g1 = lax.rem(g + grps + step, grps)
    s1 = lax.rem(s + subs + step, subs)
    return [(g, s1), (g1, s), (g1, s1)]


def basis_kernel(size, labels_hbm, perm_hbm, inverse_ref, sources_ref, shift_hbm, probe_hbm,
                 coef_ref, element_ref, labels_ref, perm_ref, shift_ref, probe_ref, inv_ref, src_ref, snap_ref,
                 grad_ref, out_ref, in_ref, side_out_ref, side_in_ref, sum_ref, m_ref, coef_out_ref, coef_in_ref,
                 small_sem, load_sem, send_sem, recv_sem, side_send_sem, side_recv_sem, coef_send_sem, coef_recv_sem):
    onward, back = neighbours(size, 1), neighbours(size, -1)
    loads = [pltpu.make_async_copy(sources_ref.at[0], src_ref, load_sem.at[0])]
    for i, (start, stop) in enumerate(CHUNKS):
        part = pl.ds(start, stop - start)
        loads.append(pltpu.make_async_copy(inverse_ref.at[0, :, part], inv_ref.at[:, part], load_sem.at[i + 1]))
    small = [pltpu.make_async_copy(source, target, small_sem.at[i]) for i, (source, target) in enumerate(
        ((labels_hbm, labels_ref), (perm_hbm, perm_ref), (shift_hbm, shift_ref), (probe_hbm, probe_ref)))]
    for load in loads[:2] + small + loads[2:]:
        load.start()
    barrier = pltpu.get_barrier_semaphore()
    for device in back:
        pl.semaphore_signal(barrier, inc=1, device_id=device, device_id_type=MESH)

    volume = 1.0 / NCELL

    def snapshots(start, stop):
        snap_ref[:, start:stop] = jnp.dot(
            src_ref[...], inv_ref[:, start:stop], preferred_element_type=f32).astype(bf)

    for load in loads[:2] + small:
        load.wait()
    for r in (0, 128):
        snap_ref[r:r + 128, 0:CHUNKS[0][1]] = jnp.dot(
            src_ref[r:r + 128, :], inv_ref[:, 0:CHUNKS[0][1]], preferred_element_type=f32).astype(bf)
    partition, inside = cell_weights()
    kappa, face = permeability(labels_ref, perm_ref, inside)
    half = [f * (0.5 * volume) for f in face]
    weights = [jnp.concatenate([h * (p + ahead(p, s)) for h, s in zip(half, STRIDES)], axis=1).astype(bf)
               for p in partition]
    probe_rows = split3(probe_ref[...])
    for load, chunk in zip(loads[2:], CHUNKS[1:]):
        load.wait()
        snapshots(*chunk)
    for d, stride in enumerate(STRIDES):
        for r in range(0, SNAP, 64):
            field = snap_ref[r:r + 64, :]
            grad_ref[r:r + 64, d * NCELL:(d + 1) * NCELL] = ahead(field, stride) - field

    row = lax.broadcasted_iota(jnp.int32, (128, 128), 0)
    col = lax.broadcasted_iota(jnp.int32, (128, 128), 1)

    def gram(corner):
        g = lax.dot_general(grad_ref[...] * weights[corner], grad_ref[...], NT, preferred_element_type=f32)
        first, below, second = g[:128, :128], g[128:, :128], g[128:, 128:]
        diagonal = jnp.sum(jnp.where(row == col, second, 0.0), axis=0, keepdims=True)
        return [jnp.where(row >= col, first, second), below, diagonal]

    def remote(sources, targets, slot, send, recv, device):
        return pltpu.make_async_remote_copy(
            src_ref=sources, dst_ref=targets.at[slot], send_sem=send.at[slot], recv_sem=recv.at[slot],
            device_id=device, device_id_type=MESH)

    def pack(slot, square, below, diagonal):
        out_ref[slot, 0:128, :] = square.astype(bf)
        out_ref[slot, 128:256, :] = below.astype(bf)
        out_ref[slot, 256:272, :] = jnp.broadcast_to(diagonal, (16, 128)).astype(bf)

    def plus(slot, square, below, diagonal):
        return (square + in_ref[slot, 0:128, :].astype(f32), below + in_ref[slot, 128:256, :].astype(f32),
                diagonal + in_ref[slot, 256:272, :].astype(f32)[0:1])

    grps, subs = size
    g, s = lax.axis_index("grp"), lax.axis_index("sub")
    parity = lax.rem(s, 2)
    far = (lax.rem(g + parity, grps), lax.rem(s + 1, subs))
    across = [remote(out_ref.at[slot], in_ref, slot, send_sem, recv_sem, device)
              for slot, device in enumerate((onward[0], onward[1], far))]
    both = gram(3), gram(2)
    pack(2, *both[0])
    pl.semaphore_wait(barrier, 3)
    across[2].start()

    @pl.when(parity == 0)
    def _():
        pack(1, *both[1])
        across[1].start()

    probed = jnp.dot(probe_rows, snap_ref[...], preferred_element_type=f32)
    probed = probed[0:8] + probed[8:16] + probed[16:24]
    heavy = kappa * volume
    loaded = jnp.concatenate([probed * (heavy * p) for p in partition], axis=0)
    side = lax.dot_general(split3(loaded), snap_ref[...], NT, preferred_element_type=f32)
    side = side[0:32] + side[32:64] + side[64:96]
    side_out_ref[...] = side
    sides = []
    for slot in (2, 1, 0):
        corner = slot + 1
        sides.append(remote(side_out_ref.at[pl.ds(8 * corner, 8)], side_in_ref, slot, side_send_sem, side_recv_sem,
                            onward[slot]))
        sides[-1].start()

    @pl.when(parity == 1)
    def _():
        across[2].wait_recv()
        pack(1, *plus(2, *both[1]))
        across[1].start()

    beside, own = gram(1), gram(0)
    pack(0, *beside)
    across[2].wait_send()
    across[1].wait_send()
    across[0].start()
    own_side = side[0:8]
    for copy in sides:
        copy.wait_recv()
    own_side = own_side + (side_in_ref[0] + side_in_ref[1] + side_in_ref[2])
    for slot in (0, 1):
        across[slot].wait_recv()
        own = plus(slot, *own)
    sum_ref[0:128, :] = own[0]
    sum_ref[128:256, :] = own[1]
    sum_ref[256:264, :] = jnp.broadcast_to(own[2], (8, 128))

    @pl.when(parity == 0)
    def _():
        across[2].wait_recv()
        sum_ref[...] = sum_ref[...] + in_ref[2, 0:264, :].astype(f32)

    square, below, diagonal = sum_ref[0:128, :], sum_ref[128:256, :], sum_ref[256:257, :]
    turned = square.T
    shift = shift_ref[...]
    m_ref[:128, :128] = jnp.where(row >= col, square, turned) + jnp.where(row == col, shift[:, :128], 0.0)
    m_ref[128:, :128] = below
    m_ref[:128, 128:256] = below.T
    m_ref[128:, 128:256] = jnp.where(
        row == col, diagonal + shift[:, 128:], jnp.where(row < col, square, turned))
    m_ref[:, N:] = jnp.concatenate([own_side, jnp.zeros((120, SNAP), f32)], axis=0).T
    eliminate(m_ref)

    solved = m_ref[:, 128:256].T[0:8]
    coef_ref[0] = solved
    own = solved.astype(bf).astype(f32)
    coef_out_ref[...] = own
    sends = []
    for slot in (2, 1, 0):
        sends.append(pltpu.make_async_remote_copy(
            src_ref=coef_out_ref, dst_ref=coef_in_ref.at[slot], send_sem=coef_send_sem.at[slot],
            recv_sem=coef_recv_sem.at[slot], device_id=back[slot], device_id_type=MESH))
        sends[-1].start()
    for send in sends:
        send.wait_recv()
    corners = jnp.concatenate([own, coef_in_ref[0], coef_in_ref[1], coef_in_ref[2]], axis=0).astype(bf)
    field = jnp.dot(corners, snap_ref[...], preferred_element_type=f32)
    field = jnp.concatenate([field[8 * c:8 * c + 8] * partition[c] for c in range(4)], axis=0)
    slopes = [ahead(field, stride) - field for stride in STRIDES]
    left = jnp.concatenate(halves(jnp.concatenate([s * f for s, f in zip(slopes, face)], axis=1)), axis=0)
    right = jnp.concatenate(halves(jnp.concatenate(slopes, axis=1)), axis=0)
    product = (lax.dot_general(left[:, :1792], right[:, :1792], NT, preferred_element_type=f32)
               + lax.dot_general(left[:, 1792:], right[:, 1792:], NT, preferred_element_type=f32))
    product = product[0:32] + product[32:64]
    element_ref[0] = (product[:, 0:32] + product[:, 32:64]) * (1.0 / (NCELL * SNAP))
    for copy in across[:1] + sides + sends:
        copy.wait_send()


def hand_out_kernel(coef_ref, element_ref, coef_out_ref, element_out_ref, sem):
    copies = [pltpu.make_async_copy(coef_ref, coef_out_ref, sem.at[0]),
              pltpu.make_async_copy(element_ref, element_out_ref, sem.at[1])]
    for copy in copies:
        copy.start()
    for copy in copies:
        copy.wait()


def local(size, phase_labels, phase_perm, local_inverse, sources, shift, probe):
    shapes = (jax.ShapeDtypeStruct((1, NBASIS, SNAP), f32), jax.ShapeDtypeStruct((1, 32, 32), f32))
    coef, element = pl.pallas_call(
        functools.partial(basis_kernel, size),
        out_shape=tuple(pltpu.VMEM(shape.shape, shape.dtype) for shape in shapes),
        in_specs=[pl.BlockSpec(memory_space=pl.ANY)] * 6,
        out_specs=(VMEM, VMEM),
        scratch_shapes=[
            pltpu.VMEM((1, NCELL), jnp.int32),
            pltpu.VMEM((1, PHASES), f32),
            pltpu.VMEM((1, SNAP), f32),
            pltpu.VMEM((NBASIS, SNAP), f32),
            pltpu.VMEM((NCELL, NCELL), bf),
            pltpu.VMEM((SNAP, NCELL), bf),
            pltpu.VMEM((SNAP, NCELL), bf),
            pltpu.VMEM((SNAP, 3 * NCELL), bf),
            pltpu.VMEM((3, PACK, 128), bf),
            pltpu.VMEM((3, PACK, 128), bf),
            pltpu.VMEM((4 * NBASIS, SNAP), f32),
            pltpu.VMEM((3, NBASIS, SNAP), f32),
            pltpu.VMEM((264, 128), f32),
            pltpu.VMEM((N, W), f32),
            pltpu.VMEM((NBASIS, SNAP), f32),
            pltpu.VMEM((3, NBASIS, SNAP), f32),
            pltpu.SemaphoreType.DMA((4,)),
            pltpu.SemaphoreType.DMA((1 + len(CHUNKS),)),
            pltpu.SemaphoreType.DMA((3,)),
            pltpu.SemaphoreType.DMA((3,)),
            pltpu.SemaphoreType.DMA((3,)),
            pltpu.SemaphoreType.DMA((3,)),
            pltpu.SemaphoreType.DMA((3,)),
            pltpu.SemaphoreType.DMA((3,)),
        ],
        compiler_params=pltpu.CompilerParams(collective_id=0, has_side_effects=True),
        name="basis",
    )(phase_labels, phase_perm.reshape(1, PHASES), local_inverse, sources, shift, probe.T)
    coef, element = pl.pallas_call(
        hand_out_kernel,
        out_shape=shapes,
        in_specs=[VMEM, VMEM],
        out_specs=(pl.BlockSpec(memory_space=pl.ANY), pl.BlockSpec(memory_space=pl.ANY)),
        scratch_shapes=[pltpu.SemaphoreType.DMA((2,))],
        name="hand_out",
    )(*(pltpu.with_memory_space_constraint(x, pltpu.VMEM) for x in (coef, element)))
    return (coef.transpose(0, 2, 1), element)


def solution(mesh):
    size = (mesh.shape["grp"], mesh.shape["sub"])
    in_specs = (
        P(("grp", "sub"), None),
        P(),
        P(("grp", "sub"), None, None),
        P(("grp", "sub"), None, None),
        P(("grp", "sub"), None),
        P(),
    )
    out_specs = (P(("grp", "sub"), None, None), P(("grp", "sub"), None, None))
    return jax.shard_map(functools.partial(local, size), mesh=mesh, in_specs=in_specs, out_specs=out_specs, check_vma=False)
```

```python
import functools
import jax
import jax.numpy as jnp
from jax import lax
from jax.experimental import pallas as pl
from jax.experimental.pallas import tpu as pltpu
from jax.sharding import PartitionSpec as P

HI = lax.Precision.HIGHEST
N = 256
NB = 16
W = 384
NBASIS = 8
bf, f32 = jnp.bfloat16, jnp.float32


def spread(group, row):
    return jnp.broadcast_to(group[row:row + 1], (8, 128))


def leaf(cols, slabs):
    row = lax.broadcasted_iota(jnp.int32, (8, 128), 0)
    cols, slabs = list(cols), list(slabs)
    for p in range(0, NB, 2):
        g, i = p // 8, p % 8
        c0, c1 = cols[p], cols[p + 1]
        a, b = spread(c0[g], i), spread(c1[g], i)
        bt, d = spread(c0[g], i + 1), spread(c1[g], i + 1)
        inv = 1.0 / (a * d - b * bt)
        a, b, bt, d = a * inv, b * inv, bt * inv, d * inv
        e0 = [x * d - y * bt for x, y in zip(c0, c1)]
        e1 = [y * a - x * b for x, y in zip(c0, c1)]
        first, second = row == i, row == i + 1
        e0[g] = jnp.where(first, -d, jnp.where(second, bt, e0[g]))
        e1[g] = jnp.where(first, b, jnp.where(second, -a, e1[g]))
        pair = (row == i) | (row == i + 1)

        def step(t):
            r0, r1 = spread(t[g], i), spread(t[g], i + 1)
            z = list(t)
            z[g] = jnp.where(pair, 0.0, t[g])
            return [x - u * r0 - v * r1 for x, u, v in zip(z, e0, e1)]

        for q in range(p + 2, NB):
            cols[q] = step(cols[q])
        slabs = [step(t) for t in slabs]
    return slabs


def halves(x):
    hi = x.astype(bf)
    return hi, (x - hi.astype(f32)).astype(bf)


def column(tile, off, q):
    return [jnp.broadcast_to(t[:, off + q:off + q + 1], (8, 128)) for t in tile]


def eliminate(m_ref):
    steps = N // NB
    tile = lambda k: (k * NB) // 128
    low8 = lambda rows: lax.broadcasted_iota(jnp.int32, (rows, 128), 1) < NBASIS

    def moved(k, pieces):
        if k == 0:
            return {0: jnp.where(low8(pieces[0].shape[0]), pieces[2], pieces[0]), 1: pieces[1]}
        if k == 8:
            return {1: jnp.where(low8(pieces[1].shape[0]), pieces[0], pieces[1])}
        return pieces

    def read(k, t):
        return [m_ref[k * NB + 8 * g:k * NB + 8 * g + 8, 128 * t:128 * t + 128] for g in range(2)]

    slab = {t: read(0, t) for t in range(3)}
    for k in range(steps):
        t0, off = tile(k), (k * NB) % 128
        cols = [column(slab[t0], off, q) for q in range(NB)]
        live = [0, 1, 2] if k == 0 else [0, 1] if k <= 8 else [1]
        new = dict(zip(live, leaf(cols, [slab[t] for t in live])))
        if k + 1 < steps:
            factor_tile = read(k + 1, t0)
            factors = [column(factor_tile, off, q) for q in range(NB)]
            nxt = {}
            for t in live:
                rows = [spread(new[t][q // 8], q % 8) for q in range(NB)]
                groups = []
                for g, start in enumerate(read(k + 1, t)):
                    parts = []
                    for c in range(0, NB, 4):
                        s = factors[c][g] * rows[c]
                        for q in range(c + 1, c + 4):
                            s = s + factors[q][g] * rows[q]
                        parts.append(s)
                    groups.append(start - ((parts[0] + parts[1]) + (parts[2] + parts[3])))
                nxt[t] = groups
            both = [moved(k, {t: nxt[t][g] for t in live}) for g in range(2)]
            slab = {t: [both[0][t], both[1][t]] for t in both[0]}
        new = {t: jnp.concatenate(new[t], axis=0) for t in live}
        hi, low = halves(jnp.concatenate([new[t] for t in live], axis=1))
        width = 128 * len(live)
        gap = lambda n: [jnp.zeros((n, width), bf)] if n else []
        right = jnp.concatenate(
            [piece for x in (hi, hi, low) for piece in gap(off) + [x] + gap(128 - off - NB)], axis=0)
        lo = live[0] * 128

        def update(r0, r1):
            if r1 <= r0:
                return
            lhi, llow = halves(m_ref[r0:r1, 128 * t0:128 * t0 + 128])
            left = jnp.concatenate([lhi, llow, lhi], axis=1)
            got = m_ref[r0:r1, lo:lo + width] - jnp.dot(left, right, preferred_element_type=f32)
            pieces = moved(k, {t: got[:, 128 * i:128 * i + 128] for i, t in enumerate(live)})
            for t in pieces:
                m_ref[r0:r1, 128 * t:128 * t + 128] = pieces[t]

        update((k + 2) * NB, N)
        update(0, k * NB)
        pieces = moved(k, new)
        for t in pieces:
            m_ref[k * NB:(k + 1) * NB, 128 * t:128 * t + 128] = pieces[t]


CELLX, CELLY, CELLZ, SNAP, NBASIS, PHASES, NCELL = 12, 12, 8, 256, 8, 3, 1152
STRIDES = (CELLY * CELLZ, CELLZ, 1)
CHUNKS = ((0, 256), (256, 768), (768, 1152))
PACK = 272
MESH = pl.DeviceIdType.MESH
NT = (((1,), (1,)), ((), ()))
VMEM = pl.BlockSpec(memory_space=pltpu.VMEM)


def ahead(field, stride):
    return pltpu.roll(field, NCELL - stride, axis=1)


def cell_weights():
    cell = lax.broadcasted_iota(jnp.int32, (1, NCELL), 1)
    run = lax.shift_right_logical(cell, 3)
    coord_x = lax.shift_right_logical(run * 683, 13)
    coord_y = run - coord_x * CELLY
    coord_z = lax.bitwise_and(cell, CELLZ - 1)
    fx = (coord_x.astype(f32) + 0.5) * (1.0 / CELLX)
    fy = (coord_y.astype(f32) + 0.5) * (1.0 / CELLY)
    partition = [(1.0 - fx) * (1.0 - fy), fx * (1.0 - fy), (1.0 - fx) * fy, fx * fy]
    inside = [coord_x < CELLX - 1, coord_y < CELLY - 1, coord_z < CELLZ - 1]
    return partition, inside


def permeability(labels_ref, perm_ref, inside):
    labels, perm = labels_ref[...], perm_ref[...]
    kappa = jnp.where(labels == 0, perm[:, 0:1], jnp.where(labels == 1, perm[:, 1:2], perm[:, 2:3]))
    face = []
    for stride, keep in zip(STRIDES, inside):
        other = ahead(kappa, stride)
        face.append(jnp.where(keep, 2.0 * kappa * other / (kappa + other), 0.0))
    return kappa, face


def split3(x):
    hi = x.astype(bf)
    rest = x - hi.astype(f32)
    mid = rest.astype(bf)
    low = (rest - mid.astype(f32)).astype(bf)
    return jnp.concatenate([hi, mid, low], axis=0)


def neighbours(axes_size, step):
    grps, subs = axes_size
    g, s = lax.axis_index("grp"), lax.axis_index("sub")
    g1 = lax.rem(g + grps + step, grps)
    s1 = lax.rem(s + subs + step, subs)
    return [(g, s1), (g1, s), (g1, s1)]


def basis_kernel(size, labels_hbm, perm_hbm, inverse_ref, sources_ref, shift_hbm, probe_hbm,
                 coef_ref, element_ref, labels_ref, perm_ref, shift_ref, probe_ref, inv_ref, src_ref, snap_ref,
                 grad_ref, out_ref, in_ref, side_out_ref, side_in_ref, sum_ref, m_ref, coef_out_ref, coef_in_ref,
                 small_sem, load_sem, send_sem, recv_sem, side_send_sem, side_recv_sem, coef_send_sem, coef_recv_sem):
    onward, back = neighbours(size, 1), neighbours(size, -1)
    loads = [pltpu.make_async_copy(sources_ref.at[0], src_ref, load_sem.at[0])]
    for i, (start, stop) in enumerate(CHUNKS):
        part = pl.ds(start, stop - start)
        loads.append(pltpu.make_async_copy(inverse_ref.at[0, :, part], inv_ref.at[:, part], load_sem.at[i + 1]))
    small = [pltpu.make_async_copy(source, target, small_sem.at[i]) for i, (source, target) in enumerate(
        ((labels_hbm, labels_ref), (perm_hbm, perm_ref), (shift_hbm, shift_ref), (probe_hbm, probe_ref)))]
    for load in loads[:2] + small + loads[2:]:
        load.start()
    barrier = pltpu.get_barrier_semaphore()
    for device in back:
        pl.semaphore_signal(barrier, inc=1, device_id=device, device_id_type=MESH)

    volume = 1.0 / NCELL

    def snapshots(start, stop):
        snap_ref[:, start:stop] = jnp.dot(
            src_ref[...], inv_ref[:, start:stop], preferred_element_type=f32).astype(bf)

    for load in loads[:2] + small:
        load.wait()
    for r in (0, 128):
        snap_ref[r:r + 128, 0:CHUNKS[0][1]] = jnp.dot(
            src_ref[r:r + 128, :], inv_ref[:, 0:CHUNKS[0][1]], preferred_element_type=f32).astype(bf)
    partition, inside = cell_weights()
    kappa, face = permeability(labels_ref, perm_ref, inside)
    half = [f * (0.5 * volume) for f in face]
    weights = [jnp.concatenate([h * (p + ahead(p, s)) for h, s in zip(half, STRIDES)], axis=1).astype(bf)
               for p in partition]
    probe_rows = split3(probe_ref[...])
    for load, chunk in zip(loads[2:], CHUNKS[1:]):
        load.wait()
        snapshots(*chunk)
    for d, stride in enumerate(STRIDES):
        for r in range(0, SNAP, 64):
            field = snap_ref[r:r + 64, :]
            grad_ref[r:r + 64, d * NCELL:(d + 1) * NCELL] = ahead(field, stride) - field

    row = lax.broadcasted_iota(jnp.int32, (128, 128), 0)
    col = lax.broadcasted_iota(jnp.int32, (128, 128), 1)

    def gram(corner):
        g = lax.dot_general(grad_ref[...] * weights[corner], grad_ref[...], NT, preferred_element_type=f32)
        first, below, second = g[:128, :128], g[128:, :128], g[128:, 128:]
        diagonal = jnp.sum(jnp.where(row == col, second, 0.0), axis=0, keepdims=True)
        return [jnp.where(row >= col, first, second), below, diagonal]

    def remote(sources, targets, slot, send, recv, device):
        return pltpu.make_async_remote_copy(
            src_ref=sources, dst_ref=targets.at[slot], send_sem=send.at[slot], recv_sem=recv.at[slot],
            device_id=device, device_id_type=MESH)

    def pack(slot, square, below, diagonal):
        out_ref[slot, 0:128, :] = square.astype(bf)
        out_ref[slot, 128:256, :] = below.astype(bf)
        out_ref[slot, 256:272, :] = jnp.broadcast_to(diagonal, (16, 128)).astype(bf)

    def plus(slot, square, below, diagonal):
        return (square + in_ref[slot, 0:128, :].astype(f32), below + in_ref[slot, 128:256, :].astype(f32),
                diagonal + in_ref[slot, 256:272, :].astype(f32)[0:1])

    grps, subs = size
    g, s = lax.axis_index("grp"), lax.axis_index("sub")
    parity = lax.rem(s, 2)
    far = (lax.rem(g + parity, grps), lax.rem(s + 1, subs))
    across = [remote(out_ref.at[slot], in_ref, slot, send_sem, recv_sem, device)
              for slot, device in enumerate((onward[0], onward[1], far))]
    both = gram(3), gram(2)
    pack(2, *both[0])
    pl.semaphore_wait(barrier, 3)
    across[2].start()

    @pl.when(parity == 0)
    def _():
        pack(1, *both[1])

    probed = jnp.dot(probe_rows, snap_ref[...], preferred_element_type=f32)
    probed = probed[0:8] + probed[8:16] + probed[16:24]
    heavy = kappa * volume
    loaded = jnp.concatenate([probed * (heavy * p) for p in partition], axis=0)
    side = lax.dot_general(split3(loaded), snap_ref[...], NT, preferred_element_type=f32)
    side = side[0:32] + side[32:64] + side[64:96]
    side_out_ref[...] = side
    sides = []
    for slot in (2, 1, 0):
        corner = slot + 1
        sides.append(remote(side_out_ref.at[pl.ds(8 * corner, 8)], side_in_ref, slot, side_send_sem, side_recv_sem,
                            onward[slot]))
        sides[-1].start()

    @pl.when(parity == 1)
    def _():
        across[2].wait_recv()
        pack(1, *plus(2, *both[1]))

    across[1].start()
    beside, own = gram(1), gram(0)
    pack(0, *beside)
    across[2].wait_send()
    across[1].wait_send()
    across[0].start()
    own_side = side[0:8]
    for copy in sides:
        copy.wait_recv()
    own_side = own_side + (side_in_ref[0] + side_in_ref[1] + side_in_ref[2])
    for slot in (0, 1):
        across[slot].wait_recv()
        own = plus(slot, *own)
    sum_ref[0:128, :] = own[0]
    sum_ref[128:256, :] = own[1]
    sum_ref[256:264, :] = jnp.broadcast_to(own[2], (8, 128))

    @pl.when(parity == 0)
    def _():
        across[2].wait_recv()
        sum_ref[...] = sum_ref[...] + in_ref[2, 0:264, :].astype(f32)

    square, below, diagonal = sum_ref[0:128, :], sum_ref[128:256, :], sum_ref[256:257, :]
    turned = square.T
    shift = shift_ref[...]
    m_ref[:128, :128] = jnp.where(row >= col, square, turned) + jnp.where(row == col, shift[:, :128], 0.0)
    m_ref[128:, :128] = below
    m_ref[:128, 128:256] = below.T
    m_ref[128:, 128:256] = jnp.where(
        row == col, diagonal + shift[:, 128:], jnp.where(row < col, square, turned))
    m_ref[:, N:] = jnp.concatenate([own_side, jnp.zeros((120, SNAP), f32)], axis=0).T
    eliminate(m_ref)

    solved = m_ref[:, 128:256].T[0:8]
    coef_ref[0] = solved
    own = solved.astype(bf).astype(f32)
    coef_out_ref[...] = own
    sends = []
    for slot in (2, 1, 0):
        sends.append(pltpu.make_async_remote_copy(
            src_ref=coef_out_ref, dst_ref=coef_in_ref.at[slot], send_sem=coef_send_sem.at[slot],
            recv_sem=coef_recv_sem.at[slot], device_id=back[slot], device_id_type=MESH))
        sends[-1].start()
    for send in sends:
        send.wait_recv()
    corners = jnp.concatenate([own, coef_in_ref[0], coef_in_ref[1], coef_in_ref[2]], axis=0).astype(bf)
    field = jnp.dot(corners, snap_ref[...], preferred_element_type=f32)
    field = jnp.concatenate([field[8 * c:8 * c + 8] * partition[c] for c in range(4)], axis=0)
    slopes = [ahead(field, stride) - field for stride in STRIDES]
    left = jnp.concatenate(halves(jnp.concatenate([s * f for s, f in zip(slopes, face)], axis=1)), axis=0)
    right = jnp.concatenate(halves(jnp.concatenate(slopes, axis=1)), axis=0)
    product = (lax.dot_general(left[:, :1792], right[:, :1792], NT, preferred_element_type=f32)
               + lax.dot_general(left[:, 1792:], right[:, 1792:], NT, preferred_element_type=f32))
    product = product[0:32] + product[32:64]
    element_ref[0] = (product[:, 0:32] + product[:, 32:64]) * (1.0 / (NCELL * SNAP))
    for copy in across[:1] + sides + sends:
        copy.wait_send()


def hand_out_kernel(coef_ref, element_ref, coef_out_ref, element_out_ref, sem):
    copies = [pltpu.make_async_copy(coef_ref, coef_out_ref, sem.at[0]),
              pltpu.make_async_copy(element_ref, element_out_ref, sem.at[1])]
    for copy in copies:
        copy.start()
    for copy in copies:
        copy.wait()


def local(size, phase_labels, phase_perm, local_inverse, sources, shift, probe):
    shapes = (jax.ShapeDtypeStruct((1, NBASIS, SNAP), f32), jax.ShapeDtypeStruct((1, 32, 32), f32))
    coef, element = pl.pallas_call(
        functools.partial(basis_kernel, size),
        out_shape=tuple(pltpu.VMEM(shape.shape, shape.dtype) for shape in shapes),
        in_specs=[pl.BlockSpec(memory_space=pl.ANY)] * 6,
        out_specs=(VMEM, VMEM),
        scratch_shapes=[
            pltpu.VMEM((1, NCELL), jnp.int32),
            pltpu.VMEM((1, PHASES), f32),
            pltpu.VMEM((1, SNAP), f32),
            pltpu.VMEM((NBASIS, SNAP), f32),
            pltpu.VMEM((NCELL, NCELL), bf),
            pltpu.VMEM((SNAP, NCELL), bf),
            pltpu.VMEM((SNAP, NCELL), bf),
            pltpu.VMEM((SNAP, 3 * NCELL), bf),
            pltpu.VMEM((3, PACK, 128), bf),
            pltpu.VMEM((3, PACK, 128), bf),
            pltpu.VMEM((4 * NBASIS, SNAP), f32),
            pltpu.VMEM((3, NBASIS, SNAP), f32),
            pltpu.VMEM((264, 128), f32),
            pltpu.VMEM((N, W), f32),
            pltpu.VMEM((NBASIS, SNAP), f32),
            pltpu.VMEM((3, NBASIS, SNAP), f32),
            pltpu.SemaphoreType.DMA((4,)),
            pltpu.SemaphoreType.DMA((1 + len(CHUNKS),)),
            pltpu.SemaphoreType.DMA((3,)),
            pltpu.SemaphoreType.DMA((3,)),
            pltpu.SemaphoreType.DMA((3,)),
            pltpu.SemaphoreType.DMA((3,)),
            pltpu.SemaphoreType.DMA((3,)),
            pltpu.SemaphoreType.DMA((3,)),
        ],
        compiler_params=pltpu.CompilerParams(collective_id=0, has_side_effects=True),
        name="basis",
    )(phase_labels, phase_perm.reshape(1, PHASES), local_inverse, sources, shift, probe.T)
    coef, element = pl.pallas_call(
        hand_out_kernel,
        out_shape=shapes,
        in_specs=[VMEM, VMEM],
        out_specs=(pl.BlockSpec(memory_space=pl.ANY), pl.BlockSpec(memory_space=pl.ANY)),
        scratch_shapes=[pltpu.SemaphoreType.DMA((2,))],
        name="hand_out",
    )(*(pltpu.with_memory_space_constraint(x, pltpu.VMEM) for x in (coef, element)))
    return (coef.transpose(0, 2, 1), element)


def solution(mesh):
    size = (mesh.shape["grp"], mesh.shape["sub"])
    in_specs = (
        P(("grp", "sub"), None),
        P(),
        P(("grp", "sub"), None, None),
        P(("grp", "sub"), None, None),
        P(("grp", "sub"), None),
        P(),
    )
    out_specs = (P(("grp", "sub"), None, None), P(("grp", "sub"), None, None))
    return jax.shard_map(functools.partial(local, size), mesh=mesh, in_specs=in_specs, out_specs=out_specs, check_vma=False)
```
